256 devices in a mesh: grp: 8 (over x, core), shard: 32 (over y, z).
Axes of the slice: x: 4, y: 4, z: 8, core: 2. Of those that a mesh axis runs over, the one named last changes fastest.
Arguments:
- cand_table: bfloat16 [4096, 512], P('grp'), may hold values from -6 to 6
- inverse: int32 [65536], P(('grp', 'shard')), may hold values from 0 to 4095
- cache_keys: bfloat16 [524288, 512], P(('grp', 'shard')), may hold values from -6 to 6
- cache_values: bfloat16 [524288, 512], P(('grp', 'shard')), may hold values from -6 to 6
- block_dest: int32 [4096, 1], P(('grp', 'shard')), may hold values from 0 to 31; in each aligned block of 16 rows (0 to 15, 16 to 31, ...) at most 2 rows name the same one
- w_in: bfloat16 [512, 1024], replicated, may hold values from -0.25 to 0.25
- w_out: bfloat16 [512, 512], replicated, may hold values from -0.25 to 0.25
Outputs:
- scored: bfloat16 [65536, 512], P(('grp', 'shard'))
The draws below stay inside these ranges and needn't reach their ends.
Inputs may be any that keep to these rules, and one draw needn't show every extreme that they name: `block_dest`: among the 16 blocks held by one device, at most 2 name the same scorer.
All inputs are finite; a program needn't handle non-finite values.
Results may differ from the reference program's by a relative error of at most 0.0082.
Values may be sent and summed in bfloat16 or wider, within the bound.
No kernel may reach another device: no remote copies, remote signals or barrier semaphores. Data moves between devices by JAX's collectives and lax.ppermute only.
A program may use at most 128 MiB of HBM per device.

```python
import math
import jax
import jax.numpy as jnp
import numpy as np
from jax import lax

D = 512
H = 8
BLK = 128
CB_DEV = 16
MOST = 2
CAND = 256
UNIQ = 4096
CAND_ALL = 65536
BLOCKS = 4096
CACHE_ROWS = 524288
N_GRP = 8
N_SHARD = 32


def plant(drawn, rng, least, largest):
    index_at = [jax.random.randint(jax.random.fold_in(rng, axis), (), 0, length) for axis, length in enumerate(drawn.shape)]
    widest = drawn.shape.index(max(drawn.shape))
    neighbour = index_at[:widest] + [(index_at[widest] + 1) % drawn.shape[widest]] + index_at[widest + 1:]
    return drawn.at[tuple(index_at)].set(least).at[tuple(neighbour)].set(largest)


def shard_levels(own_key, dims, shards, low, top_value):
    def one(dim, blocks):
        draws = jax.random.uniform(jax.random.fold_in(jax.random.fold_in(own_key, 6), dim), (blocks,), jnp.float32, low / len(shards), top_value / len(shards))
        return jnp.repeat(jnp.exp(draws), dims[dim] // blocks).reshape((-1,) + (1,) * (len(dims) - dim - 1))

    loudness = one(*shards[0])
    for cut in shards[1:]:
        loudness = loudness * one(*cut)
    return loudness


def deal_out(rng, own, number, rows, count, top, most, slope):
    order = jax.random.permutation(rng, count)
    heavy_load, usual = portions_of(count, rows * top, most, slope, True), portions_of(count, rows * top, most, slope, False)
    places = jnp.arange(count)

    def named(lengths, turn):
        used = int((lengths > 0).sum())
        fixed = max(1, used // 4)
        shifted = fixed + (places - fixed + turn * (used - fixed)) % max(1, count - fixed)
        return jnp.zeros((count,), jnp.int32).at[order[jnp.where(places < fixed, places, shifted)]].set(jnp.asarray(lengths, jnp.int32))

    lengths = jnp.where(number % 4 == 0, named(heavy_load, number // 4), named(usual, number - number // 4 - 1))
    mixed = jax.random.permutation(jax.random.fold_in(own, 3), count)
    giver, sink = mixed[0:count // 2 * 2:2], mixed[1:count // 2 * 2:2]
    slack = jnp.minimum(lengths[giver] - 1, most - lengths[sink]) // 2
    slack = jnp.where((giver == order[0]) | (sink == order[0]) | (lengths[sink] == 0), 0, jnp.maximum(slack, 0))
    shifted = jax.random.randint(jax.random.fold_in(own, 4), (count // 2,), 0, 1 << 20) % (slack + 1)
    lengths = lengths.at[giver].add(-shifted).at[sink].add(shifted)
    labels = jnp.searchsorted(jnp.cumsum(lengths), jnp.arange(rows * top), side="right").astype(jnp.int32)
    grid = labels.reshape(top, rows).T
    grid = grid[jax.random.permutation(jax.random.fold_in(own, 1), rows)]
    turn = jax.random.randint(jax.random.fold_in(own, 2), (rows, 1), 0, top)
    return jnp.take_along_axis(grid, (jnp.arange(top)[None, :] + turn) % top, axis=1)


def portions_of(amount, total, limit, skew, full):
    loads = [(1 << 20) // math.isqrt(standing ** skew) + 1 for standing in range(1, amount + 1)]
    largest = limit if full else min(limit, max(-(-total // amount), total * loads[0] // sum(loads)))
    least = 1 if total - largest >= amount - 1 else 0
    counts, surplus = [largest] + [least] * (amount - 1), total - largest - least * (amount - 1)
    while surplus > 0:
        free = [i for i in range(1, amount) if counts[i] < largest] or [i for i in range(1, amount) if counts[i] < limit]
        mass, budget = sum([loads[i] for i in free]), surplus
        for i in free:
            extra = min(limit - counts[i], max(1, budget * loads[i] // mass), surplus)
            counts[i] = counts[i] + extra
            surplus = surplus - extra
    return np.array(counts)


def gaussian(rng, shape, scale, most, pieces=(), kind=jnp.bfloat16):
    array = jax.random.normal(rng, shape, jnp.float32) * scale
    if len(pieces) > 0:
        array = shard_levels(rng, shape, pieces, -0.22, 0.18) * array
    return jnp.clip(array, min=-most, max=most).astype(kind)


def setup_inputs(seed: int = 0) -> dict:
    arg_keys = jax.random.split(jax.random.key(seed), 8)
    cand_table = gaussian(arg_keys[0], (UNIQ, D), 1.0, 6.0, ((0, 8),))
    inverse = plant(jax.random.randint(arg_keys[1], (CAND_ALL,), 0, UNIQ), jax.random.fold_in(arg_keys[1], 1), 0, UNIQ - 1).astype(jnp.int32)
    cache_keys = gaussian(arg_keys[2], (CACHE_ROWS, D), 1.0, 6.0, ((0, 256),))
    cache_values = gaussian(arg_keys[3], (CACHE_ROWS, D), 1.0, 6.0, ((0, 256),))
    block_dest_keys = jax.random.split(jax.random.fold_in(arg_keys[4], 1), BLOCKS // CB_DEV)
    block_dest_turns = jax.random.permutation(jax.random.fold_in(arg_keys[4], 3), BLOCKS // CB_DEV)
    block_dest = jax.vmap(lambda own, number: deal_out(jax.random.fold_in(arg_keys[4], 2), own, number, CB_DEV, N_SHARD, 1, MOST, 2))(block_dest_keys, block_dest_turns).reshape((BLOCKS, 1))
    w_in = gaussian(arg_keys[5], (D, 2 * D), D ** -0.5, 0.25)
    w_out = gaussian(arg_keys[6], (D, D), D ** -0.5, 0.25)
    return {"cand_table": cand_table, "inverse": inverse, "cache_keys": cache_keys, "cache_values": cache_values, "block_dest": block_dest, "w_in": w_in, "w_out": w_out}


def layer_norm(inputs):
    center = inputs - lax.optimization_barrier(jnp.mean(inputs, axis=-1, keepdims=True))
    spread = lax.optimization_barrier(jnp.mean(center * center, axis=-1, keepdims=True))
    return center * lax.rsqrt(spread + 1e-05)

def reference(cand_table, inverse, cache_keys, cache_values, block_dest, w_in, w_out):
    head_size = D // H
    score_scale = 1.0 / math.sqrt(head_size)
    device_count = N_GRP * N_SHARD
    embedded = jnp.take(cand_table, inverse, axis=0)
    normed = layer_norm(embedded.astype(jnp.float32)).astype(jnp.bfloat16)
    projected = jax.nn.silu(jnp.dot(normed, w_in, preferred_element_type=jnp.float32))
    gate_u = projected[:, :D].astype(jnp.bfloat16)
    query_low = lax.optimization_barrier(projected[:, D:].astype(jnp.bfloat16))
    queries = query_low.astype(jnp.float32).reshape(device_count, CAND, H, head_size)
    key_blocks = cache_keys.reshape(device_count, CB_DEV, BLK, H, head_size)
    value_blocks = cache_values.reshape(device_count, CB_DEV, BLK, H, head_size)
    scorer_ids = block_dest.reshape(device_count, CB_DEV)
    group_base = jnp.arange(device_count, dtype=jnp.int32) // N_SHARD * N_SHARD

    def owner_step(running, owner):
        targets = group_base[owner] + scorer_ids[owner]
        chosen = queries[targets]
        key_rows = key_blocks[owner].astype(jnp.float32)
        value_rows = value_blocks[owner].astype(jnp.float32)
        scores = jnp.einsum('bchd,bkhd->bhck', chosen, key_rows, precision=lax.Precision.HIGHEST)
        weight_low = lax.optimization_barrier(jax.nn.silu(score_scale * scores).astype(jnp.bfloat16))
        parts = jnp.einsum('bhck,bkhd->bchd', weight_low.astype(jnp.float32), value_rows, precision=lax.Precision.HIGHEST)
        return (running.at[targets].add(parts), None)
    start_sums = jnp.zeros((device_count, CAND, H, head_size), jnp.float32)
    attended, _ = lax.scan(owner_step, start_sums, jnp.arange(device_count, dtype=jnp.int32))
    attended = attended.reshape(device_count * CAND, D)
    gated_rows = (layer_norm(attended) * gate_u.astype(jnp.float32)).astype(jnp.bfloat16)
    return jnp.dot(gated_rows, w_out, preferred_element_type=jnp.float32).astype(jnp.bfloat16)
```

```python
import functools
import math

import jax
import jax.numpy as jnp
from jax import lax
from jax.experimental import pallas as pl
from jax.experimental.pallas import tpu as pltpu
from jax.sharding import PartitionSpec as P

H = 8
BLK = 128
LANES = 128
NY = 4
CORES = 2


VMEM = pl.BlockSpec(memory_space=pltpu.VMEM)
SMEM = pl.BlockSpec(memory_space=pltpu.SMEM)


def layer_norm(inputs):
    center = inputs - jnp.mean(inputs, axis=-1, keepdims=True)
    spread = jnp.mean(center * center, axis=-1, keepdims=True)
    return center * lax.rsqrt(spread + 1e-05)


def half_silu(half):
    return half + half * jnp.tanh(half)


def project_kernel(first, scale, count, *refs):
    w_ref = refs[0]
    rows_in = refs[1 : 1 + count]
    out_ref = refs[-1]
    width = w_ref.shape[0]
    at = first
    for row_ref in rows_in:
        rows = row_ref.shape[0]
        tile = math.gcd(rows, LANES)

        def step(i, carry, row_ref=row_ref, at=at, tile=tile):
            begin = pl.multiple_of(i * tile, tile)
            half = 0.5 * jnp.dot(
                row_ref[pl.ds(begin, tile), :], w_ref[:, width:], preferred_element_type=jnp.float32
            )
            query = half_silu(half).astype(jnp.bfloat16).astype(jnp.float32) * scale
            for c in range(width // LANES):
                out_ref[pl.ds(at + begin, tile), c, :] = query[:, c * LANES : (c + 1) * LANES]
            return carry

        lax.fori_loop(0, rows // tile, step, 0)
        at += rows


def project(table, first, total, pieces, w_in, scale):
    width = w_in.shape[0]
    rows = sum(p.shape[0] for p in pieces)
    ins = [w_in, *pieces]
    aliases = {}
    kernel = functools.partial(project_kernel, first, scale, len(pieces))
    if table is not None:
        aliases = {len(ins): 0}
        ins.append(table)
    return pl.pallas_call(
        kernel,
        out_shape=jax.ShapeDtypeStruct((total, width // LANES, LANES), jnp.float32),
        in_specs=[VMEM] * len(ins),
        out_specs=VMEM,
        input_output_aliases=aliases,
        cost_estimate=pl.CostEstimate(
            flops=2 * rows * width * width, bytes_accessed=rows * width * 6, transcendentals=rows * width
        ),
        compiler_params=pltpu.CompilerParams(vmem_limit_bytes=24 << 20),
        name="project",
    )(*ins)


def gate_kernel(count, index_ref, w_ref, *refs):
    pieces, out_ref = refs[:count], refs[-1]
    cand, width = out_ref.shape
    total = jnp.zeros((cand, width), jnp.float32)
    first = 0
    for piece in pieces:
        rows = piece.shape[0]
        ids = lax.broadcasted_iota(jnp.int32, (cand, rows), 1) + first
        pick = jnp.where(index_ref[...] == ids, 1.0, 0.0).astype(jnp.bfloat16)
        total = total + jnp.dot(pick, piece[...], preferred_element_type=jnp.float32)
        first += rows
    normed = total.astype(jnp.bfloat16)
    half = 0.5 * jnp.dot(normed, w_ref[:, :width], preferred_element_type=jnp.float32)
    out_ref[...] = half_silu(half).astype(jnp.bfloat16)


def gate_rows(index, pieces, w_in):
    width = w_in.shape[0]
    cand = index.shape[0]
    rows = sum(p.shape[0] for p in pieces)
    return pl.pallas_call(
        functools.partial(gate_kernel, len(pieces)),
        out_shape=jax.ShapeDtypeStruct((cand, width), jnp.bfloat16),
        in_specs=[VMEM] * (2 + len(pieces)),
        out_specs=VMEM,
        cost_estimate=pl.CostEstimate(
            flops=2 * cand * width * (rows + width), bytes_accessed=rows * width * 2, transcendentals=cand * width
        ),
        compiler_params=pltpu.CompilerParams(vmem_limit_bytes=24 << 20),
        name="gate",
    )(index[:, None], w_in, *pieces)


def attend_kernel(sizes, cand, first_row, unroll, index_ref, count_ref, block_ref, order_ref, table_ref, k_ref, v_ref, *refs):
    outs, (rows_ref, sum_ref) = refs[: len(sizes)], refs[len(sizes) :]
    rows, width = sum_ref.shape
    low = lax.broadcasted_iota(jnp.int32, (BLK, LANES), 1) < LANES // 2

    def split(tile):
        zero = jnp.zeros_like(tile)
        return jnp.concatenate([jnp.where(low, tile, zero), jnp.where(low, zero, tile)], axis=0)

    def scorer(j, carry):
        rel = order_ref[j]
        blocks = count_ref[rel]
        sum_ref[...] = jnp.zeros_like(sum_ref)

        @pl.when(blocks > 0)
        def _():
            start = rel * cand + first_row

            def fetch(i, inner_carry):
                for k in range(unroll):
                    at = i * unroll + k
                    rows_ref[at] = table_ref[index_ref[start + at]]
                return inner_carry

            lax.fori_loop(0, rows // unroll, fetch, 0)

            def one_block(slot, inner_carry):
                begin = pl.multiple_of(block_ref[2 * rel + slot] * BLK, BLK)
                for c in range(width // LANES):
                    lanes = slice(c * LANES, (c + 1) * LANES)
                    query = rows_ref[:, c, :].astype(jnp.bfloat16)
                    keys = split(k_ref[pl.ds(begin, BLK), lanes])
                    half = lax.dot_general(
                        query, keys, (((1,), (1,)), ((), ())), preferred_element_type=jnp.float32
                    )
                    weight = half_silu(half).astype(jnp.bfloat16)
                    values = split(v_ref[pl.ds(begin, BLK), lanes])
                    sum_ref[:, lanes] += jnp.dot(weight, values, preferred_element_type=jnp.float32)
                return inner_carry

            lax.fori_loop(0, blocks, one_block, 0)

        at = 0
        for out_ref, number in zip(outs, sizes):
            here = j - at

            @pl.when((here >= 0) & (here < number))
            def _(out_ref=out_ref, here=here):
                out_ref[here] = sum_ref[...].astype(out_ref.dtype)

            at += number
        return carry

    lax.fori_loop(0, sum(sizes), scorer, 0)


def attend(plan, first_row, rows, cand, index, count, block, table, keys, values):
    width = keys.shape[1]
    sizes = tuple(len(p) for p in plan)
    scorers = sum(sizes)
    order = jnp.asarray([rel for p in plan for rel in p], jnp.int32)
    return pl.pallas_call(
        functools.partial(attend_kernel, sizes, cand, first_row, 16 if rows % 16 == 0 else 8),
        out_shape=[jax.ShapeDtypeStruct((n, rows, width), jnp.bfloat16) for n in sizes],
        in_specs=[SMEM] * 4 + [VMEM] * 3,
        out_specs=[VMEM] * len(sizes),
        scratch_shapes=[
            pltpu.VMEM((rows, width // LANES, LANES), jnp.float32),
            pltpu.VMEM((rows, width), jnp.float32),
        ],
        cost_estimate=pl.CostEstimate(
            flops=scorers * rows * BLK * width * 8,
            bytes_accessed=scorers * rows * width * 4,
            transcendentals=scorers * rows * BLK * H // 2,
        ),
        compiler_params=pltpu.CompilerParams(vmem_limit_bytes=28 << 20),
        name="attend",
    )(index, count, block, order, table, keys, values)


def add(*terms):
    total = terms[0].astype(jnp.float32)
    for term in terms[1:]:
        total = total + term.astype(jnp.float32)
    return total


def add_low(*terms):
    return add(*terms).astype(jnp.bfloat16)


def on_device(cand_table, inverse, cache_keys, cache_values, block_dest, w_in, w_out):
    width = w_out.shape[0]
    cand = inverse.shape[0]
    groups, peers = lax.axis_size("grp"), lax.axis_size("shard")
    nx, nz = groups // CORES, peers // NY
    g, s = lax.axis_index("grp"), lax.axis_index("shard")
    my_x, my_core, my_y, my_z = g // CORES, g % CORES, s // nz, s % nz
    part_rows = cand_table.shape[0]
    total_rows = groups * part_rows
    half_part = part_rows // 2

    def x_shift(value, k):
        return lax.ppermute(
            value, "grp", [(x * CORES + c, (x + k) % nx * CORES + c) for x in range(nx) for c in range(CORES)]
        )

    def swap(value):
        return lax.ppermute(
            value, "grp", [(x * CORES + c, x * CORES + 1 - c) for x in range(nx) for c in range(CORES)]
        )

    def z_shift(value, k):
        return lax.ppermute(
            value, "shard", [(y * nz + z, y * nz + (z + k) % nz) for y in range(NY) for z in range(nz)]
        )

    def y_shift(value, k):
        return lax.ppermute(
            value, "shard", [(y * nz + z, (y + k) % NY * nz + z) for y in range(NY) for z in range(nz)]
        )

    normed = layer_norm(cand_table.astype(jnp.float32)).astype(jnp.bfloat16)
    top, bottom = normed[:half_part], normed[half_part:]
    next_top, prev_bottom = x_shift(top, -1), x_shift(bottom, 1)
    next_bottom, prev_top = x_shift(bottom, -1), x_shift(top, 1)
    far_top, far_bottom = x_shift(next_top, -1), x_shift(prev_bottom, 1)

    wanted = inverse[None, None, :]
    step = 1
    while step < nz:
        wanted = jnp.concatenate([wanted, z_shift(wanted, -step)], axis=1)
        step *= 2
    step = 1
    while step < NY:
        wanted = jnp.concatenate([wanted, y_shift(wanted, -step)], axis=0)
        step *= 2
    owner = wanted // part_rows
    place = (owner // CORES - my_x) % nx * CORES + (owner % CORES + my_core) % CORES
    relative = place * part_rows + wanted % part_rows
    index = relative.reshape(-1)

    destination = block_dest[:, 0]
    blocks = destination.shape[0]
    block_ids = jnp.arange(blocks, dtype=jnp.int32)
    earlier = (destination[:, None] == destination[None, :]) & (block_ids[None, :] < block_ids[:, None])
    rank = jnp.sum(earlier.astype(jnp.int32), axis=1)
    rel_dest = (destination // nz - my_y) % NY * nz + (destination % nz - my_z) % nz
    slots = jnp.arange(2 * peers, dtype=jnp.int32)
    match = (rel_dest * 2 + rank)[None, :] == slots[:, None]
    block = jnp.sum(jnp.where(match, block_ids[None, :], 0), axis=1)
    count = jnp.sum(
        (rel_dest[None, :] == jnp.arange(peers, dtype=jnp.int32)[:, None]).astype(jnp.int32), axis=1
    )

    scale = 0.5 / math.sqrt(width // H)
    near = [normed, swap(normed)]
    ahead = [next_top, next_bottom, swap(next_top), swap(next_bottom)]
    behind = [prev_top, prev_bottom, swap(prev_top), swap(prev_bottom)]
    far = [far_top, far_bottom, swap(far_top), swap(far_bottom)]
    chip = CORES * part_rows
    table = project(None, 0, total_rows, near, w_in, scale)
    table = project(table, 1 * chip, total_rows, ahead, w_in, scale)
    table = project(table, 3 * chip, total_rows, behind, w_in, scale)
    table = project(table, 2 * chip, total_rows, far, w_in, scale)

    z_rows = cand // 2
    y_rows = cand - z_rows

    def attend_z(*offsets):
        plan = []
        for dz in offsets:
            plan += [[dz, nz + dz], [2 * nz + dz, 3 * nz + dz]]
        return attend(plan, 0, z_rows, cand, index, count, block, table, cache_keys, cache_values)

    def attend_y(*offsets):
        plan = []
        for dy in offsets:
            plan += [[dy * nz + dz for dz in range(nz // 2)], [dy * nz + dz for dz in range(nz // 2, nz)]]
        return attend(plan, z_rows, y_rows, cand, index, count, block, table, cache_keys, cache_values)

    za, zb, ya, yb = {}, {}, {}, {}
    za[4], zb[4] = attend_z(4)
    ya[2], yb[2] = attend_y(2)
    za[3], zb[3], za[5], zb[5] = attend_z(3, 5)
    ya[1], yb[1], ya[3], yb[3] = attend_y(1, 3)
    za[2], zb[2], za[6], zb[6] = attend_z(2, 6)
    za[1], zb[1], za[7], zb[7] = attend_z(1, 7)
    za[0], zb[0] = attend_z(0)
    ya[0], yb[0] = attend_y(0)

    up_a, up_b, down_b, down_a = za[4], zb[3], zb[4], za[5]
    up_a, down_b = z_shift(up_a, 1), z_shift(down_b, -1)
    up_a, down_b = add_low(up_a, za[3]), add_low(down_b, zb[5])
    for k in (2, 1):
        up_b, down_a = add_low(z_shift(up_b, 1), zb[k]), add_low(z_shift(down_a, -1), za[8 - k])
        up_a, down_b = add_low(z_shift(up_a, 1), za[k]), add_low(z_shift(down_b, -1), zb[8 - k])
    up_b, down_a = z_shift(up_b, 1), z_shift(down_a, -1)
    up_a, down_b = z_shift(up_a, 1), z_shift(down_b, -1)

    plus_a, minus_b = y_shift(ya[2], 1), y_shift(yb[2], -1)
    plus_b, minus_a = y_shift(yb[1], 1), y_shift(ya[3], -1)
    plus_a, minus_b = y_shift(add_low(plus_a, ya[1]), 1), y_shift(add_low(minus_b, yb[3]), -1)

    hz = z_rows // 2

    def z_sum(dy, rows):
        if dy < 2:
            return [za[0][dy, rows], up_a[dy, rows], down_a[dy, rows]]
        return [zb[0][dy - 2, rows], up_b[dy - 2, rows], down_b[dy - 2, rows]]

    first, last = slice(0, hz), slice(hz, z_rows)
    far_first = y_shift(add_low(*z_sum(2, first)), 1)
    far_last = y_shift(add_low(*z_sum(2, last)), -1)
    plus_last = y_shift(add_low(*z_sum(1, last)), 1)
    minus_first = y_shift(add_low(*z_sum(3, first)), -1)
    plus_first = y_shift(add_low(far_first, *z_sum(1, first)), 1)
    minus_last = y_shift(add_low(far_last, *z_sum(3, last)), -1)
    own = [
        add(*z_sum(0, first), plus_first, minus_first),
        add(*z_sum(0, last), plus_last, minus_last),
    ]

    hy = y_rows // 2
    half_z = nz // 2

    def y_sum(dz, rows):
        if dz < half_z:
            return [ya[0][dz, rows], plus_a[dz, rows], minus_a[dz, rows]]
        return [yb[0][dz - half_z, rows], plus_b[dz - half_z, rows], minus_b[dz - half_z, rows]]

    first, last = slice(0, hy), slice(hy, y_rows)
    up_first = add_low(*y_sum(4, first))
    down_last = add_low(*y_sum(4, last))
    up_last = add_low(*y_sum(3, last))
    down_first = add_low(*y_sum(5, first))
    for k in (3, 2, 1):
        up_first = add_low(z_shift(up_first, 1), *y_sum(k, first))
        down_last = add_low(z_shift(down_last, -1), *y_sum(8 - k, last))
        if k > 1:
            up_last = add_low(z_shift(up_last, 1), *y_sum(k - 1, last))
            down_first = add_low(z_shift(down_first, -1), *y_sum(9 - k, first))
    up_last, down_first = z_shift(up_last, 1), z_shift(down_first, -1)
    up_first, down_last = z_shift(up_first, 1), z_shift(down_last, -1)
    own += [
        add(*y_sum(0, first), up_first, down_first),
        add(*y_sum(0, last), up_last, down_last),
    ]

    gate_u = gate_rows(relative[0, 0], near + ahead + far + behind, w_in)
    attended = jnp.concatenate(own, axis=0)
    gated_rows = (layer_norm(attended) * gate_u.astype(jnp.float32)).astype(jnp.bfloat16)
    return jnp.dot(gated_rows, w_out, preferred_element_type=jnp.float32).astype(jnp.bfloat16)


def solution(mesh):
    in_specs = (
        P("grp", None),
        P(("grp", "shard")),
        P(("grp", "shard"), None),
        P(("grp", "shard"), None),
        P(("grp", "shard"), None),
        P(),
        P(),
    )
    out_specs = P(("grp", "shard"), None)
    return jax.shard_map(
        on_device, mesh=mesh, in_specs=in_specs, out_specs=out_specs, check_vma=False
    )
```

```python
import functools
import math

import jax
import jax.numpy as jnp
from jax import lax
from jax.experimental import pallas as pl
from jax.experimental.pallas import tpu as pltpu
from jax.sharding import PartitionSpec as P

H = 8
BLK = 128
LANES = 128
NY = 4
CORES = 2
TILE = 256


VMEM = pl.BlockSpec(memory_space=pltpu.VMEM)
SMEM = pl.BlockSpec(memory_space=pltpu.SMEM)


def layer_norm(inputs):
    center = inputs - jnp.mean(inputs, axis=-1, keepdims=True)
    spread = jnp.mean(center * center, axis=-1, keepdims=True)
    return center * lax.rsqrt(spread + 1e-05)


def half_silu(half):
    return half + half * jnp.tanh(half)


def norm_kernel(in_ref, out_ref):
    out_ref[...] = layer_norm(in_ref[...].astype(jnp.float32)).astype(out_ref.dtype)


def norm(rows):
    return pl.pallas_call(
        norm_kernel,
        out_shape=jax.ShapeDtypeStruct(rows.shape, jnp.bfloat16),
        in_specs=[VMEM],
        out_specs=VMEM,
        compiler_params=pltpu.CompilerParams(vmem_limit_bytes=8 << 20),
        name="norm",
    )(rows)


def project_kernel(first, scale, count, *refs):
    w_ref = refs[0]
    rows_in = refs[1 : 1 + count]
    out_ref = refs[-1]
    width = w_ref.shape[0]
    cuts = width // LANES
    at = first
    for row_ref in rows_in:
        rows = row_ref.shape[0]
        tile = math.gcd(rows, TILE)

        def step(i, carry, row_ref=row_ref, at=at, tile=tile):
            begin = pl.multiple_of(i * tile, tile)
            half = 0.5 * jnp.dot(
                row_ref[pl.ds(begin, tile), :], w_ref[:, width:], preferred_element_type=jnp.float32
            )
            query = half_silu(half).astype(jnp.bfloat16).astype(jnp.float32) * scale
            for c in range(cuts):
                out_ref[pl.ds((at + begin) * cuts + c, tile, stride=cuts), :] = query[:, c * LANES : (c + 1) * LANES]
            return carry

        lax.fori_loop(0, rows // tile, step, 0)
        at += rows


def project(table, first, total, pieces, w_in, scale):
    width = w_in.shape[0]
    rows = sum(p.shape[0] for p in pieces)
    ins = [w_in, *pieces]
    aliases = {}
    kernel = functools.partial(project_kernel, first, scale, len(pieces))
    if table is not None:
        aliases = {len(ins): 0}
        ins.append(table)
    return pl.pallas_call(
        kernel,
        out_shape=jax.ShapeDtypeStruct((total * width // LANES, LANES), jnp.float32),
        in_specs=[VMEM] * len(ins),
        out_specs=VMEM,
        input_output_aliases=aliases,
        cost_estimate=pl.CostEstimate(
            flops=2 * rows * width * width, bytes_accessed=rows * width * 6, transcendentals=rows * width
        ),
        compiler_params=pltpu.CompilerParams(vmem_limit_bytes=8 << 20),
        name="project",
    )(*ins)


def gate_kernel(count, index_ref, w_ref, *refs):
    pieces, out_ref = refs[:count], refs[-1]
    cand, width = out_ref.shape
    total = jnp.zeros((cand, width), jnp.float32)
    first = 0
    index = jnp.broadcast_to(index_ref[...], (LANES, cand)).T[:, :1]
    for piece in pieces:
        rows = piece.shape[0]
        ids = lax.broadcasted_iota(jnp.int32, (cand, rows), 1) + first
        pick = jnp.where(index == ids, 1.0, 0.0).astype(jnp.bfloat16)
        total = total + jnp.dot(pick, piece[...], preferred_element_type=jnp.float32)
        first += rows
    normed = total.astype(jnp.bfloat16)
    half = 0.5 * jnp.dot(normed, w_ref[:, :width], preferred_element_type=jnp.float32)
    out_ref[...] = half_silu(half).astype(jnp.bfloat16)


def gate_rows(index, pieces, w_in):
    width = w_in.shape[0]
    cand = index.shape[0]
    rows = sum(p.shape[0] for p in pieces)
    return pl.pallas_call(
        functools.partial(gate_kernel, len(pieces)),
        out_shape=jax.ShapeDtypeStruct((cand, width), jnp.bfloat16),
        in_specs=[VMEM] * (2 + len(pieces)),
        out_specs=VMEM,
        cost_estimate=pl.CostEstimate(
            flops=2 * cand * width * (rows + width), bytes_accessed=rows * width * 2, transcendentals=cand * width
        ),
        compiler_params=pltpu.CompilerParams(vmem_limit_bytes=8 << 20),
        name="gate",
    )(index[None, :], w_in, *pieces)


def attend_kernel(sizes, unroll, index_ref, count_ref, block_ref, order_ref, table_ref, k_ref, v_ref, *refs):
    outs, (rows_ref, query_ref, sum_ref) = refs[: len(sizes)], refs[len(sizes) :]
    rows, width = sum_ref.shape
    cuts = width // LANES
    low = lax.broadcasted_iota(jnp.int32, (BLK, LANES), 1) < LANES // 2

    def split(tile):
        zero = jnp.zeros_like(tile)
        return jnp.concatenate([jnp.where(low, tile, zero), jnp.where(low, zero, tile)], axis=0)

    def task(j, carry):
        scorer = order_ref[2 * j]
        start = order_ref[2 * j + 1]
        blocks = count_ref[scorer]
        sum_ref[...] = jnp.zeros_like(sum_ref)

        @pl.when(blocks > 0)
        def _():
            def fetch(i, inner_carry):
                begin = start + i * unroll
                to = i * (unroll * cuts)
                for k in range(unroll):
                    at = pl.multiple_of(index_ref[begin + k], cuts)
                    rows_ref[pl.ds(pl.multiple_of(to + k * cuts, cuts), cuts), :] = table_ref[pl.ds(at, cuts), :]
                return inner_carry

            lax.fori_loop(0, rows // unroll, fetch, 0)
            for c in range(cuts):
                query_ref[:, c * LANES : (c + 1) * LANES] = rows_ref[pl.ds(c, rows, stride=cuts), :].astype(jnp.bfloat16)

            def one_block(slot, inner_carry):
                begin = pl.multiple_of(block_ref[2 * scorer + slot] * BLK, BLK)
                for c in range(cuts):
                    lanes = slice(c * LANES, (c + 1) * LANES)
                    keys = split(k_ref[pl.ds(begin, BLK), lanes])
                    half = lax.dot_general(
                        query_ref[:, lanes], keys, (((1,), (1,)), ((), ())), preferred_element_type=jnp.float32
                    )
                    weight = half_silu(half).astype(jnp.bfloat16)
                    values = split(v_ref[pl.ds(begin, BLK), lanes])
                    sum_ref[:, lanes] += jnp.dot(weight, values, preferred_element_type=jnp.float32)
                return inner_carry

            lax.fori_loop(0, blocks, one_block, 0)

        at = 0
        for out_ref, number in zip(outs, sizes):
            here = j - at

            @pl.when((here >= 0) & (here < number))
            def _(out_ref=out_ref, here=here):
                out_ref[here] = sum_ref[...].astype(out_ref.dtype)

            at += number
        return carry

    lax.fori_loop(0, sum(sizes), task, 0)


def attend(sizes, rows, index, count, block, order, table, keys, values):
    width = keys.shape[1]
    number = sum(sizes)
    return pl.pallas_call(
        functools.partial(attend_kernel, tuple(sizes), 16 if rows % 16 == 0 else 8),
        out_shape=[jax.ShapeDtypeStruct((n, rows, width), jnp.bfloat16) for n in sizes],
        in_specs=[SMEM] * 4 + [VMEM] * 3,
        out_specs=[VMEM] * len(sizes),
        scratch_shapes=[
            pltpu.VMEM((rows * width // LANES, LANES), jnp.float32),
            pltpu.VMEM((rows, width), jnp.bfloat16),
            pltpu.VMEM((rows, width), jnp.float32),
        ],
        cost_estimate=pl.CostEstimate(
            flops=number * rows * BLK * width * 8,
            bytes_accessed=number * rows * width * 4,
            transcendentals=number * rows * BLK * H // 2,
        ),
        compiler_params=pltpu.CompilerParams(vmem_limit_bytes=6 << 20),
        name="attend",
    )(index, count, block, order, table, keys, values)


def finish_kernel(halves, *refs):
    gate_ref, w_ref, out_ref = refs[-3], refs[-2], refs[-1]
    at, first = 0, 0
    for number in halves:
        total = refs[at][...].astype(jnp.float32)
        for ref in refs[at + 1 : at + number]:
            total = total + ref[...].astype(jnp.float32)
        rows = total.shape[0]
        gated = (layer_norm(total) * gate_ref[first : first + rows, :].astype(jnp.float32)).astype(jnp.bfloat16)
        out_ref[first : first + rows, :] = jnp.dot(
            gated, w_ref[...], preferred_element_type=jnp.float32
        ).astype(out_ref.dtype)
        at += number
        first += rows


def finish(halves, gate_u, w_out):
    terms = [t for half in halves for t in half]
    return pl.pallas_call(
        functools.partial(finish_kernel, [len(half) for half in halves]),
        out_shape=jax.ShapeDtypeStruct(gate_u.shape, jnp.bfloat16),
        in_specs=[VMEM] * (len(terms) + 2),
        out_specs=VMEM,
        compiler_params=pltpu.CompilerParams(vmem_limit_bytes=8 << 20),
        name="finish",
    )(*terms, gate_u, w_out)


def add(*terms):
    total = terms[0].astype(jnp.float32)
    for term in terms[1:]:
        total = total + term.astype(jnp.float32)
    return total.astype(jnp.bfloat16)


def compute(cand_table, inverse, cache_keys, cache_values, block_dest, w_in, w_out):
    width = w_out.shape[0]
    cand = inverse.shape[0]
    groups, peers = lax.axis_size("grp"), lax.axis_size("shard")
    nx, nz = groups // CORES, peers // NY
    g, s = lax.axis_index("grp"), lax.axis_index("shard")
    part_rows = cand_table.shape[0]
    total_rows = groups * part_rows
    half_part = part_rows // 2
    cuts = width // LANES

    def x_shift(value, k):
        return lax.ppermute(
            value, "grp", [(x * CORES + c, (x + k) % nx * CORES + c) for x in range(nx) for c in range(CORES)]
        )

    def swap(value):
        return lax.ppermute(
            value, "grp", [(x * CORES + c, x * CORES + 1 - c) for x in range(nx) for c in range(CORES)]
        )

    def z_shift(value, k):
        return lax.ppermute(
            value, "shard", [(y * nz + z, y * nz + (z + k) % nz) for y in range(NY) for z in range(nz)]
        )

    def y_shift(value, k):
        return lax.ppermute(
            value, "shard", [(y * nz + z, (y + k) % NY * nz + z) for y in range(NY) for z in range(nz)]
        )

    normed = norm(cand_table)
    ahead = x_shift(normed, -1)
    behind = x_shift(normed, 1)
    other = swap(normed)
    far_top = x_shift(ahead[:half_part], -1)
    far_bottom = x_shift(behind[half_part:], 1)

    wanted = inverse
    step = 1
    while step < nz:
        wanted = jnp.concatenate([wanted, z_shift(wanted, -step)])
        step *= 2
    step = 1
    while step < NY:
        wanted = jnp.concatenate([wanted, y_shift(wanted, -step)])
        step *= 2

    def arrival(row):
        owner = row // part_rows
        place = (owner // CORES + nx - g // CORES) & (nx - 1)
        return (place * CORES + ((owner ^ g) & (CORES - 1))) * part_rows + row % part_rows

    index = arrival(wanted) * cuts
    own_relative = arrival(inverse)

    destination = block_dest[:, 0]
    blocks = destination.shape[0]
    block_ids = jnp.arange(blocks, dtype=jnp.int32)
    earlier = (destination[:, None] == destination[None, :]) & (block_ids[None, :] < block_ids[:, None])
    rank = jnp.sum(earlier.astype(jnp.int32), axis=1)
    rel_dest = ((destination // nz + NY - s // nz) & (NY - 1)) * nz + ((destination + nz - s) & (nz - 1))
    slots = jnp.arange(2 * peers, dtype=jnp.int32)
    match = (rel_dest * 2 + rank)[None, :] == slots[:, None]
    block = jnp.sum(jnp.where(match, block_ids[None, :], 0), axis=1)
    count = jnp.sum(
        (rel_dest[None, :] == jnp.arange(peers, dtype=jnp.int32)[:, None]).astype(jnp.int32), axis=1
    )

    scale = 0.5 / math.sqrt(width // H)
    chip = CORES * part_rows
    near_rows = [normed, other]
    table = project(None, 0, total_rows, near_rows, w_in, scale)
    ahead_rows = [ahead, swap(ahead)]
    behind_rows = [behind, swap(behind)]
    table = project(table, 1 * chip, total_rows, ahead_rows, w_in, scale)
    table = project(table, 3 * chip, total_rows, behind_rows, w_in, scale)
    far_rows = [far_top, far_bottom, swap(far_top), swap(far_bottom)]
    table = project(table, 2 * chip, total_rows, far_rows, w_in, scale)

    half = cand // 2
    half_z = nz // 2
    z_of = lambda dz, dys=range(NY): [(dy, dz, 0) for dy in dys]
    y_of = lambda dy, dzs=range(nz): [(dy, dz, half) for dz in dzs]
    calls = [
        [z_of(4, (0, 1)), z_of(4, (2, 3)), y_of(2, range(half_z)), y_of(2, range(half_z, nz))],
        [z_of(3), z_of(5), y_of(1), y_of(3)],
        [z_of(2), z_of(6), z_of(1), z_of(7), z_of(0), y_of(0)],
    ]
    flat = [t for call in calls for piece in call for t in piece]
    order = [v for dy, dz, start in flat for v in (dy * nz + dz, (dy * nz + dz) * cand + start)]
    parts, at = [], 0
    for call in calls:
        sizes = [len(piece) for piece in call]
        mine = jnp.asarray(order[2 * at : 2 * (at + sum(sizes))], jnp.int32)
        parts += attend(sizes, half, index, count, block, mine, table, cache_keys, cache_values)
        at += sum(sizes)
    z4a, z4b, y2a, y2b, z3, z5, y1, y3, z2, z6, z1, z7, z0, y0 = parts

    two = NY // 2
    up = z_shift(z4a, 1)
    down = z_shift(z4b, -1)
    far_y_up = y_shift(y2a, 1)
    far_y_down = y_shift(y2b, -1)
    up = jnp.concatenate([add(up, z3[:two]), z3[two:]], axis=0)
    down = jnp.concatenate([z5[:two], add(down, z5[two:])], axis=0)
    up = z_shift(up, 1)
    down = z_shift(down, -1)
    y_up = jnp.concatenate([add(far_y_up, y1[:half_z]), y1[half_z:]], axis=0)
    y_down = jnp.concatenate([y3[:half_z], add(far_y_down, y3[half_z:])], axis=0)
    y_up = y_shift(y_up, 1)
    y_down = y_shift(y_down, -1)
    up, down = z_shift(add(up, z2), 1), z_shift(add(down, z6), -1)
    up, down = z_shift(add(up, z1), 1), z_shift(add(down, z7), -1)

    quarter = half // 2

    def y_sum(dz, rows):
        return [y0[dz, rows], y_up[dz, rows], y_down[dz, rows]]

    first, last = slice(0, quarter), slice(quarter, half)
    both = slice(0, half)
    y_first = z_shift(add(*y_sum(4, first)), 1)
    y_last = z_shift(add(*y_sum(4, last)), -1)
    y_first = z_shift(jnp.concatenate([add(y_first, *y_sum(3, first)), add(*y_sum(3, last))], axis=0), 1)
    y_last = z_shift(jnp.concatenate([add(*y_sum(5, first)), add(y_last, *y_sum(5, last))], axis=0), -1)
    for k in (2, 1):
        y_first = z_shift(add(y_first, *y_sum(k, both)), 1)
        y_last = z_shift(add(y_last, *y_sum(nz - k, both)), -1)

    def z_sum(dy, rows):
        return [z0[dy, rows], up[dy, rows], down[dy, rows]]

    z_first = y_shift(add(*z_sum(2, first)), 1)
    z_last = y_shift(add(*z_sum(2, last)), -1)
    z_first = y_shift(jnp.concatenate([add(z_first, *z_sum(1, first)), add(*z_sum(1, last))], axis=0), 1)
    z_last = y_shift(jnp.concatenate([add(*z_sum(3, first)), add(z_last, *z_sum(3, last))], axis=0), -1)

    gate_u = gate_rows(own_relative, near_rows + ahead_rows + far_rows + behind_rows, w_in)
    return finish(
        [[*z_sum(0, both), z_first, z_last], [*y_sum(0, both), y_first, y_last]], gate_u, w_out
    )


def solution(mesh):
    in_specs = (
        P("grp", None),
        P(("grp", "shard")),
        P(("grp", "shard"), None),
        P(("grp", "shard"), None),
        P(("grp", "shard"), None),
        P(),
        P(),
    )
    out_specs = P(("grp", "shard"), None)
    return jax.shard_map(compute, mesh=mesh, in_specs=in_specs, out_specs=out_specs, check_vma=False)
```

```python
import functools
import math

import jax
import jax.numpy as jnp
from jax import lax
from jax.experimental import pallas as pl
from jax.experimental.pallas import tpu as pltpu
from jax.sharding import PartitionSpec as P

H = 8
BLK = 128
LANES = 128
NY = 4
CORES = 2
TILE = 128


VMEM = pl.BlockSpec(memory_space=pltpu.VMEM)
SMEM = pl.BlockSpec(memory_space=pltpu.SMEM)


def layer_norm(inputs):
    center = inputs - jnp.mean(inputs, axis=-1, keepdims=True)
    spread = jnp.mean(center * center, axis=-1, keepdims=True)
    return center * lax.rsqrt(spread + 1e-05)


def half_silu(half):
    return half + half * jnp.tanh(half)


def norm_kernel(in_ref, out_ref):
    tile = math.gcd(in_ref.shape[0], TILE)

    def step(i, carry):
        rows = pl.ds(pl.multiple_of(i * tile, tile), tile)
        out_ref[rows, :] = layer_norm(in_ref[rows, :].astype(jnp.float32)).astype(out_ref.dtype)
        return carry

    lax.fori_loop(0, in_ref.shape[0] // tile, step, 0)


def norm(rows):
    return pl.pallas_call(
        norm_kernel,
        out_shape=jax.ShapeDtypeStruct(rows.shape, jnp.bfloat16),
        in_specs=[VMEM],
        out_specs=VMEM,
        compiler_params=pltpu.CompilerParams(vmem_limit_bytes=8 << 20),
        name="norm",
    )(rows)


def project_kernel(first, scale, count, *refs):
    w_ref = refs[0]
    rows_in = refs[1 : 1 + count]
    out_ref = refs[-1]
    width = w_ref.shape[0]
    cuts = width // LANES
    at = first
    for row_ref in rows_in:
        rows = row_ref.shape[0]
        tile = math.gcd(rows, TILE)

        def step(i, carry, row_ref=row_ref, at=at, tile=tile):
            begin = pl.multiple_of(i * tile, tile)
            half = 0.5 * jnp.dot(
                row_ref[pl.ds(begin, tile), :], w_ref[:, width:], preferred_element_type=jnp.float32
            )
            query = half_silu(half).astype(jnp.bfloat16).astype(jnp.float32) * scale
            for c in range(cuts):
                out_ref[pl.ds((at + begin) * cuts + c, tile, stride=cuts), :] = query[:, c * LANES : (c + 1) * LANES]
            return carry

        lax.fori_loop(0, rows // tile, step, 0)
        at += rows


def project(table, first, total, pieces, w_in, scale):
    width = w_in.shape[0]
    rows = sum(p.shape[0] for p in pieces)
    ins = [w_in, *pieces]
    aliases = {}
    kernel = functools.partial(project_kernel, first, scale, len(pieces))
    if table is not None:
        aliases = {len(ins): 0}
        ins.append(table)
    return pl.pallas_call(
        kernel,
        out_shape=jax.ShapeDtypeStruct((total * width // LANES, LANES), jnp.float32),
        in_specs=[VMEM] * len(ins),
        out_specs=VMEM,
        input_output_aliases=aliases,
        cost_estimate=pl.CostEstimate(
            flops=2 * rows * width * width, bytes_accessed=rows * width * 6, transcendentals=rows * width
        ),
        compiler_params=pltpu.CompilerParams(vmem_limit_bytes=8 << 20),
        name="project",
    )(*ins)


def gate_kernel(count, index_ref, w_ref, *refs):
    pieces, out_ref = refs[:count], refs[-1]
    cand, width = out_ref.shape
    total = jnp.zeros((cand, width), jnp.float32)
    first = 0
    index = jnp.broadcast_to(index_ref[...], (LANES, cand)).T[:, :1]
    for piece in pieces:
        rows = piece.shape[0]
        ids = lax.broadcasted_iota(jnp.int32, (cand, rows), 1) + first
        pick = jnp.where(index == ids, 1.0, 0.0).astype(jnp.bfloat16)
        total = total + jnp.dot(pick, piece[...], preferred_element_type=jnp.float32)
        first += rows
    normed = total.astype(jnp.bfloat16)
    half = 0.5 * jnp.dot(normed, w_ref[:, :width], preferred_element_type=jnp.float32)
    out_ref[...] = half_silu(half).astype(jnp.bfloat16)


def gate_rows(index, pieces, w_in):
    width = w_in.shape[0]
    cand = index.shape[0]
    rows = sum(p.shape[0] for p in pieces)
    return pl.pallas_call(
        functools.partial(gate_kernel, len(pieces)),
        out_shape=jax.ShapeDtypeStruct((cand, width), jnp.bfloat16),
        in_specs=[VMEM] * (2 + len(pieces)),
        out_specs=VMEM,
        cost_estimate=pl.CostEstimate(
            flops=2 * cand * width * (rows + width), bytes_accessed=rows * width * 2, transcendentals=cand * width
        ),
        compiler_params=pltpu.CompilerParams(vmem_limit_bytes=8 << 20),
        name="gate",
    )(index[None, :], w_in, *pieces)


def attend_kernel(sizes, unroll, index_ref, count_ref, block_ref, order_ref, table_ref, k_ref, v_ref, *refs):
    outs, (rows_ref, query_ref, sum_ref) = refs[: len(sizes)], refs[len(sizes) :]
    rows, width = sum_ref.shape
    cuts = width // LANES
    low = lax.broadcasted_iota(jnp.int32, (BLK, LANES), 1) < LANES // 2

    def split(tile):
        zero = jnp.zeros_like(tile)
        return jnp.concatenate([jnp.where(low, tile, zero), jnp.where(low, zero, tile)], axis=0)

    def task(j, carry):
        scorer = order_ref[2 * j]
        start = order_ref[2 * j + 1]
        blocks = count_ref[scorer]
        sum_ref[...] = jnp.zeros_like(sum_ref)

        @pl.when(blocks > 0)
        def _():
            def fetch(i, inner_carry):
                begin = start + i * unroll
                to = i * (unroll * cuts)
                for k in range(unroll):
                    at = pl.multiple_of(index_ref[begin + k], cuts)
                    rows_ref[pl.ds(pl.multiple_of(to + k * cuts, cuts), cuts), :] = table_ref[pl.ds(at, cuts), :]
                return inner_carry

            lax.fori_loop(0, rows // unroll, fetch, 0)
            for c in range(cuts):
                query_ref[:, c * LANES : (c + 1) * LANES] = rows_ref[pl.ds(c, rows, stride=cuts), :].astype(jnp.bfloat16)

            def one_block(slot, inner_carry):
                begin = pl.multiple_of(block_ref[2 * scorer + slot] * BLK, BLK)
                for c in range(cuts):
                    lanes = slice(c * LANES, (c + 1) * LANES)
                    keys = split(k_ref[pl.ds(begin, BLK), lanes])
                    half = lax.dot_general(
                        query_ref[:, lanes], keys, (((1,), (1,)), ((), ())), preferred_element_type=jnp.float32
                    )
                    weight = half_silu(half).astype(jnp.bfloat16)
                    values = split(v_ref[pl.ds(begin, BLK), lanes])
                    sum_ref[:, lanes] += jnp.dot(weight, values, preferred_element_type=jnp.float32)
                return inner_carry

            lax.fori_loop(0, blocks, one_block, 0)

        at = 0
        for out_ref, number in zip(outs, sizes):
            here = j - at

            @pl.when((here >= 0) & (here < number))
            def _(out_ref=out_ref, here=here):
                out_ref[here] = sum_ref[...].astype(out_ref.dtype)

            at += number
        return carry

    lax.fori_loop(0, sum(sizes), task, 0)


def attend(sizes, rows, index, count, block, order, table, keys, values):
    width = keys.shape[1]
    number = sum(sizes)
    return pl.pallas_call(
        functools.partial(attend_kernel, tuple(sizes), math.gcd(rows, 32)),
        out_shape=[jax.ShapeDtypeStruct((n, rows, width), jnp.bfloat16) for n in sizes],
        in_specs=[SMEM] * 4 + [VMEM] * 3,
        out_specs=[VMEM] * len(sizes),
        scratch_shapes=[
            pltpu.VMEM((rows * width // LANES, LANES), jnp.float32),
            pltpu.VMEM((rows, width), jnp.bfloat16),
            pltpu.VMEM((rows, width), jnp.float32),
        ],
        cost_estimate=pl.CostEstimate(
            flops=number * rows * BLK * width * 8,
            bytes_accessed=number * rows * width * 4,
            transcendentals=number * rows * BLK * H // 2,
        ),
        compiler_params=pltpu.CompilerParams(vmem_limit_bytes=6 << 20),
        name="attend",
    )(index, count, block, order, table, keys, values)


def finish_kernel(halves, *refs):
    gate_ref, w_ref, out_ref = refs[-3], refs[-2], refs[-1]
    at, first = 0, 0
    for number in halves:
        total = refs[at][...].astype(jnp.float32)
        for ref in refs[at + 1 : at + number]:
            total = total + ref[...].astype(jnp.float32)
        rows = total.shape[0]
        gated = (layer_norm(total) * gate_ref[first : first + rows, :].astype(jnp.float32)).astype(jnp.bfloat16)
        out_ref[first : first + rows, :] = jnp.dot(
            gated, w_ref[...], preferred_element_type=jnp.float32
        ).astype(out_ref.dtype)
        at += number
        first += rows


def finish(halves, gate_u, w_out):
    terms = [t for half in halves for t in half]
    return pl.pallas_call(
        functools.partial(finish_kernel, [len(half) for half in halves]),
        out_shape=jax.ShapeDtypeStruct(gate_u.shape, jnp.bfloat16),
        in_specs=[VMEM] * (len(terms) + 2),
        out_specs=VMEM,
        compiler_params=pltpu.CompilerParams(vmem_limit_bytes=8 << 20),
        name="finish",
    )(*terms, gate_u, w_out)


def add(*terms):
    total = terms[0].astype(jnp.float32)
    for term in terms[1:]:
        total = total + term.astype(jnp.float32)
    return total.astype(jnp.bfloat16)


def compute(cand_table, inverse, cache_keys, cache_values, block_dest, w_in, w_out):
    width = w_out.shape[0]
    cand = inverse.shape[0]
    groups, peers = lax.axis_size("grp"), lax.axis_size("shard")
    nx, nz = groups // CORES, peers // NY
    g, s = lax.axis_index("grp"), lax.axis_index("shard")
    part_rows = cand_table.shape[0]
    total_rows = groups * part_rows
    half_part = part_rows // 2
    cuts = width // LANES

    def x_shift(value, k):
        return lax.ppermute(
            value, "grp", [(x * CORES + c, (x + k) % nx * CORES + c) for x in range(nx) for c in range(CORES)]
        )

    def swap(value):
        return lax.ppermute(
            value, "grp", [(x * CORES + c, x * CORES + 1 - c) for x in range(nx) for c in range(CORES)]
        )

    def z_shift(value, k):
        return lax.ppermute(
            value, "shard", [(y * nz + z, y * nz + (z + k) % nz) for y in range(NY) for z in range(nz)]
        )

    def y_shift(value, k):
        return lax.ppermute(
            value, "shard", [(y * nz + z, (y + k) % NY * nz + z) for y in range(NY) for z in range(nz)]
        )

    normed = norm(cand_table)
    ahead = x_shift(normed, -1)
    behind = x_shift(normed, 1)
    other = swap(normed)
    wanted = inverse
    step = 1
    while step < nz:
        wanted = jnp.concatenate([wanted, z_shift(wanted, -step)])
        step *= 2
    wanted, ahead, behind = lax.optimization_barrier((wanted, ahead, behind))
    far_top = x_shift(ahead[:half_part], -1)
    far_bottom = x_shift(behind[half_part:], 1)
    ahead_rows = [ahead, swap(ahead)]
    behind_rows = [behind, swap(behind)]
    step = 1
    while step < NY:
        wanted = jnp.concatenate([wanted, y_shift(wanted, -step)])
        step *= 2

    def arrival(row):
        owner = row // part_rows
        place = (owner // CORES + nx - g // CORES) & (nx - 1)
        return (place * CORES + ((owner ^ g) & (CORES - 1))) * part_rows + row % part_rows

    index = arrival(wanted) * cuts
    own_relative = arrival(inverse)

    destination = block_dest[:, 0]
    blocks = destination.shape[0]
    block_ids = jnp.arange(blocks, dtype=jnp.int32)
    earlier = (destination[:, None] == destination[None, :]) & (block_ids[None, :] < block_ids[:, None])
    rank = jnp.sum(earlier.astype(jnp.int32), axis=1)
    rel_dest = ((destination // nz + NY - s // nz) & (NY - 1)) * nz + ((destination + nz - s) & (nz - 1))
    slots = jnp.arange(2 * peers, dtype=jnp.int32)
    match = (rel_dest * 2 + rank)[None, :] == slots[:, None]
    block = jnp.sum(jnp.where(match, block_ids[None, :], 0), axis=1)
    count = jnp.sum(
        (rel_dest[None, :] == jnp.arange(peers, dtype=jnp.int32)[:, None]).astype(jnp.int32), axis=1
    )

    scale = 0.5 / math.sqrt(width // H)
    chip = CORES * part_rows
    near_rows = [normed, other]
    table = project(None, 0, total_rows, near_rows, w_in, scale)
    table = project(table, 1 * chip, total_rows, ahead_rows, w_in, scale)
    table = project(table, 3 * chip, total_rows, behind_rows, w_in, scale)
    far_rows = [far_top, far_bottom, swap(far_top), swap(far_bottom)]
    table = project(table, 2 * chip, total_rows, far_rows, w_in, scale)

    half = cand // 2
    half_z = nz // 2
    z_of = lambda dz, dys=range(NY): [(dy, dz, 0) for dy in dys]
    y_of = lambda dy, dzs=range(nz): [(dy, dz, half) for dz in dzs]
    calls = [
        [z_of(4, (0, 1)), z_of(4, (2, 3)), y_of(2, range(half_z)), y_of(2, range(half_z, nz))],
        [z_of(3), z_of(5)],
        [y_of(1), y_of(3)],
        [z_of(2), z_of(6)],
        [z_of(1), z_of(7), z_of(0), y_of(0)],
    ]
    flat = [t for call in calls for piece in call for t in piece]
    order = [v for dy, dz, start in flat for v in (dy * nz + dz, (dy * nz + dz) * cand + start)]
    parts, at = [], 0
    for call in calls:
        sizes = [len(piece) for piece in call]
        mine = jnp.asarray(order[2 * at : 2 * (at + sum(sizes))], jnp.int32)
        parts += attend(sizes, half, index, count, block, mine, table, cache_keys, cache_values)
        at += sum(sizes)
    z4a, z4b, y2a, y2b, z3, z5, y1, y3, z2, z6, z1, z7, z0, y0 = parts

    two = NY // 2
    up = z_shift(z4a, 1)
    down = z_shift(z4b, -1)
    far_y_up = y_shift(y2a, 1)
    far_y_down = y_shift(y2b, -1)
    up = jnp.concatenate([add(up, z3[:two]), z3[two:]], axis=0)
    down = jnp.concatenate([z5[:two], add(down, z5[two:])], axis=0)
    up = z_shift(up, 1)
    down = z_shift(down, -1)
    y_up = jnp.concatenate([add(far_y_up, y1[:half_z]), y1[half_z:]], axis=0)
    y_down = jnp.concatenate([y3[:half_z], add(far_y_down, y3[half_z:])], axis=0)
    y_up = y_shift(y_up, 1)
    y_down = y_shift(y_down, -1)
    up = z_shift(add(up, z2), 1)
    down = z_shift(add(down, z6), -1)
    up = z_shift(add(up, z1), 1)
    down = z_shift(add(down, z7), -1)

    quarter = half // 2

    def y_sum(dz, rows):
        return [y0[dz, rows], y_up[dz, rows], y_down[dz, rows]]

    first, last = slice(0, quarter), slice(quarter, half)
    both = slice(0, half)
    y_first = z_shift(add(*y_sum(4, first)), 1)
    y_last = z_shift(add(*y_sum(4, last)), -1)
    y_first = z_shift(jnp.concatenate([add(y_first, *y_sum(3, first)), add(*y_sum(3, last))], axis=0), 1)
    y_last = z_shift(jnp.concatenate([add(*y_sum(5, first)), add(y_last, *y_sum(5, last))], axis=0), -1)
    for k in (2, 1):
        y_first = z_shift(add(y_first, *y_sum(k, both)), 1)
        y_last = z_shift(add(y_last, *y_sum(nz - k, both)), -1)

    def z_sum(dy, rows):
        return [z0[dy, rows], up[dy, rows], down[dy, rows]]

    z_first = y_shift(add(*z_sum(2, first)), 1)
    z_last = y_shift(add(*z_sum(2, last)), -1)
    z_first = y_shift(jnp.concatenate([add(z_first, *z_sum(1, first)), add(*z_sum(1, last))], axis=0), 1)
    z_last = y_shift(jnp.concatenate([add(*z_sum(3, first)), add(z_last, *z_sum(3, last))], axis=0), -1)

    gate_u = gate_rows(own_relative, near_rows + ahead_rows + far_rows + behind_rows, w_in)
    return finish(
        [[*z_sum(0, both), z_first, z_last], [*y_sum(0, both), y_first, y_last]], gate_u, w_out
    )


def solution(mesh):
    in_specs = (
        P("grp", None),
        P(("grp", "shard")),
        P(("grp", "shard"), None),
        P(("grp", "shard"), None),
        P(("grp", "shard"), None),
        P(),
        P(),
    )
    out_specs = P(("grp", "shard"), None)
    return jax.shard_map(compute, mesh=mesh, in_specs=in_specs, out_specs=out_specs, check_vma=False)
```

```python
import functools
import math

import jax
import jax.numpy as jnp
from jax import lax
from jax.experimental import pallas as pl
from jax.experimental.pallas import tpu as pltpu
from jax.sharding import PartitionSpec as P

H = 8
BLK = 128
LANES = 128
NY = 4
CORES = 2
TILE = 256


VMEM = pl.BlockSpec(memory_space=pltpu.VMEM)
SMEM = pl.BlockSpec(memory_space=pltpu.SMEM)


def layer_norm(inputs):
    center = inputs - jnp.mean(inputs, axis=-1, keepdims=True)
    spread = jnp.mean(center * center, axis=-1, keepdims=True)
    return center * lax.rsqrt(spread + 1e-05)


def half_silu(half):
    return half + half * jnp.tanh(half)


def norm_kernel(in_ref, out_ref):
    tile = math.gcd(in_ref.shape[0], TILE)

    def step(i, carry):
        rows = pl.ds(pl.multiple_of(i * tile, tile), tile)
        out_ref[rows, :] = layer_norm(in_ref[rows, :].astype(jnp.float32)).astype(out_ref.dtype)
        return carry

    lax.fori_loop(0, in_ref.shape[0] // tile, step, 0)


def norm(rows):
    return pl.pallas_call(
        norm_kernel,
        out_shape=jax.ShapeDtypeStruct(rows.shape, jnp.bfloat16),
        in_specs=[VMEM],
        out_specs=VMEM,
        compiler_params=pltpu.CompilerParams(vmem_limit_bytes=8 << 20),
        name="norm",
    )(rows)


def pack_rows(pieces, rows_ref):
    at = 0
    for piece in pieces:
        tile = math.gcd(piece.shape[0], LANES)

        def step(i, carry, piece=piece, at=at, tile=tile):
            begin = pl.multiple_of(i * tile, tile)
            rows_ref[pl.ds(at + begin, tile), :] = piece[pl.ds(begin, tile), :]
            return carry

        lax.fori_loop(0, piece.shape[0] // tile, step, 0)
        at += piece.shape[0]


def project_kernel(first, scale, count, *refs):
    w_ref = refs[0]
    out_ref, rows_ref = refs[-2], refs[-1]
    rows, width = rows_ref.shape
    cuts = width // LANES
    tile = math.gcd(rows, TILE)
    pack_rows(refs[1 : 1 + count], rows_ref)

    def step(i, carry):
        begin = pl.multiple_of(i * tile, tile)
        half = 0.5 * jnp.dot(
            rows_ref[pl.ds(begin, tile), :], w_ref[:, width:], preferred_element_type=jnp.float32
        )
        query = half_silu(half).astype(jnp.bfloat16).astype(jnp.float32) * scale
        for c in range(cuts):
            out_ref[pl.ds((first + begin) * cuts + c, tile, stride=cuts), :] = query[:, c * LANES : (c + 1) * LANES]
        return carry

    lax.fori_loop(0, rows // tile, step, 0)


def project(table, first, total, pieces, w_in, scale):
    width = w_in.shape[0]
    rows = sum(p.shape[0] for p in pieces)
    ins = [w_in, *pieces]
    aliases = {}
    kernel = functools.partial(project_kernel, first, scale, len(pieces))
    if table is not None:
        aliases = {len(ins): 0}
        ins.append(table)
    return pl.pallas_call(
        kernel,
        out_shape=jax.ShapeDtypeStruct((total * width // LANES, LANES), jnp.float32),
        in_specs=[VMEM] * len(ins),
        out_specs=VMEM,
        scratch_shapes=[pltpu.VMEM((rows, width), jnp.bfloat16)],
        input_output_aliases=aliases,
        cost_estimate=pl.CostEstimate(
            flops=2 * rows * width * width, bytes_accessed=rows * width * 6, transcendentals=rows * width
        ),
        compiler_params=pltpu.CompilerParams(vmem_limit_bytes=8 << 20),
        name="project",
    )(*ins)


def gate_kernel(count, index_ref, w_ref, *refs):
    pieces, out_ref, rows_ref, sum_ref = refs[:count], refs[-3], refs[-2], refs[-1]
    cand, width = out_ref.shape
    tile = math.gcd(rows_ref.shape[0], TILE)
    pack_rows(pieces, rows_ref)
    sum_ref[...] = jnp.zeros_like(sum_ref)
    index = jnp.broadcast_to(index_ref[...], (LANES, cand)).T[:, :1]
    ids = lax.broadcasted_iota(jnp.int32, (cand, tile), 1)

    def step(i, carry):
        begin = pl.multiple_of(i * tile, tile)
        pick = jnp.where(index - begin == ids, 1.0, 0.0).astype(jnp.bfloat16)
        sum_ref[...] += jnp.dot(pick, rows_ref[pl.ds(begin, tile), :], preferred_element_type=jnp.float32)
        return carry

    lax.fori_loop(0, rows_ref.shape[0] // tile, step, 0)
    normed = sum_ref[...].astype(jnp.bfloat16)
    half = 0.5 * jnp.dot(normed, w_ref[:, :width], preferred_element_type=jnp.float32)
    out_ref[...] = half_silu(half).astype(jnp.bfloat16)


def gate_rows(index, pieces, w_in):
    width = w_in.shape[0]
    cand = index.shape[0]
    rows = sum(p.shape[0] for p in pieces)
    return pl.pallas_call(
        functools.partial(gate_kernel, len(pieces)),
        out_shape=jax.ShapeDtypeStruct((cand, width), jnp.bfloat16),
        in_specs=[VMEM] * (2 + len(pieces)),
        out_specs=VMEM,
        scratch_shapes=[pltpu.VMEM((rows, width), jnp.bfloat16), pltpu.VMEM((cand, width), jnp.float32)],
        cost_estimate=pl.CostEstimate(
            flops=2 * cand * width * (rows + width), bytes_accessed=rows * width * 2, transcendentals=cand * width
        ),
        compiler_params=pltpu.CompilerParams(vmem_limit_bytes=8 << 20),
        name="gate",
    )(index[None, :], w_in, *pieces)


def attend_kernel(sizes, unroll, index_ref, count_ref, block_ref, order_ref, table_ref, k_ref, v_ref, *refs):
    outs, (rows_ref, query_ref, sum_ref, weight_ref) = refs[: len(sizes)], refs[len(sizes) :]
    rows, width = sum_ref.shape
    cuts = width // LANES
    low = lax.broadcasted_iota(jnp.int32, (BLK, LANES), 1) < LANES // 2

    def split(tile):
        zero = jnp.zeros_like(tile)
        return jnp.concatenate([jnp.where(low, tile, zero), jnp.where(low, zero, tile)], axis=0)

    def task(j, carry):
        scorer = order_ref[2 * j]
        start = order_ref[2 * j + 1]
        blocks = count_ref[scorer]
        sum_ref[...] = jnp.zeros_like(sum_ref)

        @pl.when(blocks > 0)
        def _():
            def fetch(i, inner_carry):
                begin = start + i * unroll
                to = i * (unroll * cuts)
                for k in range(unroll):
                    at = pl.multiple_of(index_ref[begin + k], cuts)
                    rows_ref[pl.ds(pl.multiple_of(to + k * cuts, cuts), cuts), :] = table_ref[pl.ds(at, cuts), :]
                return inner_carry

            lax.fori_loop(0, rows // unroll, fetch, 0)
            for c in range(cuts):
                query_ref[:, c * LANES : (c + 1) * LANES] = rows_ref[pl.ds(c, rows, stride=cuts), :].astype(jnp.bfloat16)

            def one_block(slot, inner_carry):
                begin = pl.multiple_of(block_ref[2 * scorer + slot] * BLK, BLK)
                for c in range(cuts):
                    lanes = slice(c * LANES, (c + 1) * LANES)
                    keys = split(k_ref[pl.ds(begin, BLK), lanes])
                    half = lax.dot_general(
                        query_ref[:, lanes], keys, (((1,), (1,)), ((), ())), preferred_element_type=jnp.float32
                    )
                    weight_ref[c] = half_silu(half).astype(jnp.bfloat16)
                for c in range(cuts):
                    lanes = slice(c * LANES, (c + 1) * LANES)
                    values = split(v_ref[pl.ds(begin, BLK), lanes])
                    sum_ref[:, lanes] += jnp.dot(weight_ref[c], values, preferred_element_type=jnp.float32)
                return inner_carry

            lax.fori_loop(0, blocks, one_block, 0)

        at = 0
        for out_ref, number in zip(outs, sizes):
            here = j - at

            @pl.when((here >= 0) & (here < number))
            def _(out_ref=out_ref, here=here):
                out_ref[here] = sum_ref[...].astype(out_ref.dtype)

            at += number
        return carry

    lax.fori_loop(0, sum(sizes), task, 0)


def attend(sizes, rows, index, count, block, order, table, keys, values):
    width = keys.shape[1]
    number = sum(sizes)
    return pl.pallas_call(
        functools.partial(attend_kernel, tuple(sizes), math.gcd(rows, 32)),
        out_shape=[jax.ShapeDtypeStruct((n, rows, width), jnp.bfloat16) for n in sizes],
        in_specs=[SMEM] * 4 + [VMEM] * 3,
        out_specs=[VMEM] * len(sizes),
        scratch_shapes=[
            pltpu.VMEM((rows * width // LANES, LANES), jnp.float32),
            pltpu.VMEM((rows, width), jnp.bfloat16),
            pltpu.VMEM((rows, width), jnp.float32),
            pltpu.VMEM((width // LANES, rows, 2 * BLK), jnp.bfloat16),
        ],
        cost_estimate=pl.CostEstimate(
            flops=number * rows * BLK * width * 8,
            bytes_accessed=number * rows * width * 4,
            transcendentals=number * rows * BLK * H // 2,
        ),
        compiler_params=pltpu.CompilerParams(vmem_limit_bytes=6 << 20),
        name="attend",
    )(index, count, block, order, table, keys, values)


def finish_kernel(halves, *refs):
    gate_ref, w_ref, out_ref = refs[-3], refs[-2], refs[-1]
    at, first = 0, 0
    for number in halves:
        total = refs[at][...].astype(jnp.float32)
        for ref in refs[at + 1 : at + number]:
            total = total + ref[...].astype(jnp.float32)
        rows = total.shape[0]
        gated = (layer_norm(total) * gate_ref[first : first + rows, :].astype(jnp.float32)).astype(jnp.bfloat16)
        out_ref[first : first + rows, :] = jnp.dot(
            gated, w_ref[...], preferred_element_type=jnp.float32
        ).astype(out_ref.dtype)
        at += number
        first += rows


def finish(halves, gate_u, w_out):
    terms = [t for half in halves for t in half]
    return pl.pallas_call(
        functools.partial(finish_kernel, [len(half) for half in halves]),
        out_shape=jax.ShapeDtypeStruct(gate_u.shape, jnp.bfloat16),
        in_specs=[VMEM] * (len(terms) + 2),
        out_specs=VMEM,
        compiler_params=pltpu.CompilerParams(vmem_limit_bytes=8 << 20),
        name="finish",
    )(*terms, gate_u, w_out)


def add(*terms):
    total = terms[0].astype(jnp.float32)
    for term in terms[1:]:
        total = total + term.astype(jnp.float32)
    return total.astype(jnp.bfloat16)


def compute(cand_table, inverse, cache_keys, cache_values, block_dest, w_in, w_out):
    width = w_out.shape[0]
    cand = inverse.shape[0]
    groups, peers = lax.axis_size("grp"), lax.axis_size("shard")
    nx, nz = groups // CORES, peers // NY
    g, s = lax.axis_index("grp"), lax.axis_index("shard")
    part_rows = cand_table.shape[0]
    total_rows = groups * part_rows
    half_part = part_rows // 2
    cuts = width // LANES

    def x_shift(value, k):
        return lax.ppermute(
            value, "grp", [(x * CORES + c, (x + k) % nx * CORES + c) for x in range(nx) for c in range(CORES)]
        )

    def swap(value):
        return lax.ppermute(
            value, "grp", [(x * CORES + c, x * CORES + 1 - c) for x in range(nx) for c in range(CORES)]
        )

    def z_shift(value, k):
        return lax.ppermute(
            value, "shard", [(y * nz + z, y * nz + (z + k) % nz) for y in range(NY) for z in range(nz)]
        )

    def y_shift(value, k):
        return lax.ppermute(
            value, "shard", [(y * nz + z, (y + k) % NY * nz + z) for y in range(NY) for z in range(nz)]
        )

    normed = norm(cand_table)
    ahead = x_shift(normed, -1)
    behind = x_shift(normed, 1)
    other = swap(normed)
    wanted = inverse
    step = 1
    while step < nz:
        wanted = jnp.concatenate([wanted, z_shift(wanted, -step)])
        step *= 2
    wanted, ahead, behind = lax.optimization_barrier((wanted, ahead, behind))
    far_top = x_shift(ahead[:half_part], -1)
    far_bottom = x_shift(behind[half_part:], 1)
    ahead_rows = [ahead, swap(ahead)]
    behind_rows = [behind, swap(behind)]
    step = 1
    while step < NY:
        wanted = jnp.concatenate([wanted, y_shift(wanted, -step)])
        step *= 2

    def arrival(row):
        owner = row // part_rows
        place = (owner // CORES + nx - g // CORES) & (nx - 1)
        return (place * CORES + ((owner ^ g) & (CORES - 1))) * part_rows + row % part_rows

    index = arrival(wanted) * cuts
    own_relative = arrival(inverse)

    destination = block_dest[:, 0]
    blocks = destination.shape[0]
    block_ids = jnp.arange(blocks, dtype=jnp.int32)
    earlier = (destination[:, None] == destination[None, :]) & (block_ids[None, :] < block_ids[:, None])
    rank = jnp.sum(earlier.astype(jnp.int32), axis=1)
    rel_dest = ((destination // nz + NY - s // nz) & (NY - 1)) * nz + ((destination + nz - s) & (nz - 1))
    slots = jnp.arange(2 * peers, dtype=jnp.int32)
    match = (rel_dest * 2 + rank)[None, :] == slots[:, None]
    block = jnp.sum(jnp.where(match, block_ids[None, :], 0), axis=1)
    count = jnp.sum(
        (rel_dest[None, :] == jnp.arange(peers, dtype=jnp.int32)[:, None]).astype(jnp.int32), axis=1
    )

    scale = 0.5 / math.sqrt(width // H)
    chip = CORES * part_rows
    near_rows = [normed, other]
    table = project(None, 0, total_rows, near_rows, w_in, scale)
    table = project(table, 1 * chip, total_rows, ahead_rows, w_in, scale)
    table = project(table, 3 * chip, total_rows, behind_rows, w_in, scale)
    far_rows = [far_top, far_bottom, swap(far_top), swap(far_bottom)]
    table = project(table, 2 * chip, total_rows, far_rows, w_in, scale)

    half = cand // 2
    half_z = nz // 2
    z_of = lambda dz, dys=range(NY): [(dy, dz, 0) for dy in dys]
    y_of = lambda dy, dzs=range(nz): [(dy, dz, half) for dz in dzs]
    calls = [
        [z_of(4, (0, 1)), z_of(4, (2, 3)), y_of(2, range(half_z)), y_of(2, range(half_z, nz))],
        [z_of(3), z_of(5)],
        [y_of(1), y_of(3)],
        [z_of(2), z_of(6)],
        [z_of(1), z_of(7), z_of(0), y_of(0)],
    ]
    flat = [t for call in calls for piece in call for t in piece]
    order = [v for dy, dz, start in flat for v in (dy * nz + dz, (dy * nz + dz) * cand + start)]
    parts, at = [], 0
    for call in calls:
        sizes = [len(piece) for piece in call]
        mine = jnp.asarray(order[2 * at : 2 * (at + sum(sizes))], jnp.int32)
        parts += attend(sizes, half, index, count, block, mine, table, cache_keys, cache_values)
        at += sum(sizes)
    z4a, z4b, y2a, y2b, z3, z5, y1, y3, z2, z6, z1, z7, z0, y0 = parts

    two = NY // 2
    up = z_shift(z4a, 1)
    down = z_shift(z4b, -1)
    far_y_up = y_shift(y2a, 1)
    far_y_down = y_shift(y2b, -1)
    up = jnp.concatenate([add(up, z3[:two]), z3[two:]], axis=0)
    down = jnp.concatenate([z5[:two], add(down, z5[two:])], axis=0)
    up = z_shift(up, 1)
    down = z_shift(down, -1)
    y_up = jnp.concatenate([add(far_y_up, y1[:half_z]), y1[half_z:]], axis=0)
    y_down = jnp.concatenate([y3[:half_z], add(far_y_down, y3[half_z:])], axis=0)
    y_up = y_shift(y_up, 1)
    y_down = y_shift(y_down, -1)
    up = z_shift(add(up, z2), 1)
    down = z_shift(add(down, z6), -1)
    up = z_shift(add(up, z1), 1)
    down = z_shift(add(down, z7), -1)

    quarter = half // 2

    def y_sum(dz, rows):
        return [y0[dz, rows], y_up[dz, rows], y_down[dz, rows]]

    first, last = slice(0, quarter), slice(quarter, half)
    both = slice(0, half)
    y_first = z_shift(add(*y_sum(4, first)), 1)
    y_last = z_shift(add(*y_sum(4, last)), -1)
    y_first = z_shift(jnp.concatenate([add(y_first, *y_sum(3, first)), add(*y_sum(3, last))], axis=0), 1)
    y_last = z_shift(jnp.concatenate([add(*y_sum(5, first)), add(y_last, *y_sum(5, last))], axis=0), -1)
    for k in (2, 1):
        y_first = z_shift(add(y_first, *y_sum(k, both)), 1)
        y_last = z_shift(add(y_last, *y_sum(nz - k, both)), -1)

    def z_sum(dy, rows):
        return [z0[dy, rows], up[dy, rows], down[dy, rows]]

    z_first = y_shift(add(*z_sum(2, first)), 1)
    z_last = y_shift(add(*z_sum(2, last)), -1)
    z_first = y_shift(jnp.concatenate([add(z_first, *z_sum(1, first)), add(*z_sum(1, last))], axis=0), 1)
    z_last = y_shift(jnp.concatenate([add(*z_sum(3, first)), add(z_last, *z_sum(3, last))], axis=0), -1)

    gate_u = gate_rows(own_relative, near_rows + ahead_rows + far_rows + behind_rows, w_in)
    return finish(
        [[*z_sum(0, both), z_first, z_last], [*y_sum(0, both), y_first, y_last]], gate_u, w_out
    )


def solution(mesh):
    in_specs = (
        P("grp", None),
        P(("grp", "shard")),
        P(("grp", "shard"), None),
        P(("grp", "shard"), None),
        P(("grp", "shard"), None),
        P(),
        P(),
    )
    out_specs = P(("grp", "shard"), None)
    return jax.shard_map(compute, mesh=mesh, in_specs=in_specs, out_specs=out_specs, check_vma=False)
```

```python
import functools
import math

import jax
import jax.numpy as jnp
from jax import lax
from jax.experimental import pallas as pl
from jax.experimental.pallas import tpu as pltpu
from jax.sharding import PartitionSpec as P

H = 8
BLK = 128
LANES = 128
NY = 4
CORES = 2
TILE = 256


VMEM = pl.BlockSpec(memory_space=pltpu.VMEM)
SMEM = pl.BlockSpec(memory_space=pltpu.SMEM)


def layer_norm(inputs):
    center = inputs - jnp.mean(inputs, axis=-1, keepdims=True)
    spread = jnp.mean(center * center, axis=-1, keepdims=True)
    return center * lax.rsqrt(spread + 1e-05)


def half_silu(half):
    return half + half * jnp.tanh(half)


def norm_kernel(in_ref, out_ref):
    tile = math.gcd(in_ref.shape[0], TILE)

    def step(i, carry):
        rows = pl.ds(pl.multiple_of(i * tile, tile), tile)
        out_ref[rows, :] = layer_norm(in_ref[rows, :].astype(jnp.float32)).astype(out_ref.dtype)
        return carry

    lax.fori_loop(0, in_ref.shape[0] // tile, step, 0)


def norm(rows):
    return pl.pallas_call(
        norm_kernel,
        out_shape=jax.ShapeDtypeStruct(rows.shape, jnp.bfloat16),
        in_specs=[VMEM],
        out_specs=VMEM,
        compiler_params=pltpu.CompilerParams(vmem_limit_bytes=8 << 20),
        name="norm",
    )(rows)


def pack_rows(pieces, rows_ref):
    at = 0
    for piece in pieces:
        tile = math.gcd(piece.shape[0], LANES)

        def step(i, carry, piece=piece, at=at, tile=tile):
            begin = pl.multiple_of(i * tile, tile)
            rows_ref[pl.ds(at + begin, tile), :] = piece[pl.ds(begin, tile), :]
            return carry

        lax.fori_loop(0, piece.shape[0] // tile, step, 0)
        at += piece.shape[0]


def project_kernel(first, scale, count, unrolled, *refs):
    w_ref = refs[0]
    out_ref, rows_ref = refs[-2], refs[-1]
    rows, width = rows_ref.shape
    cuts = width // LANES
    tile = math.gcd(refs[1].shape[0], TILE)

    def one_tile(values, to):
        half = 0.5 * jnp.dot(values, w_ref[:, width:], preferred_element_type=jnp.float32)
        query = half_silu(half).astype(jnp.bfloat16).astype(jnp.float32) * scale
        for c in range(cuts):
            out_ref[pl.ds((first + to) * cuts + c, tile, stride=cuts), :] = query[:, c * LANES : (c + 1) * LANES]

    if unrolled:
        at = 0
        for piece in refs[1 : 1 + count]:
            for begin in range(0, piece.shape[0], tile):
                one_tile(piece[begin : begin + tile, :], at + begin)
            at += piece.shape[0]
        return
    pack_rows(refs[1 : 1 + count], rows_ref)

    def step(i, carry):
        begin = pl.multiple_of(i * tile, tile)
        one_tile(rows_ref[pl.ds(begin, tile), :], begin)
        return carry

    lax.fori_loop(0, rows // tile, step, 0)


def project(table, first, total, pieces, w_in, scale, unrolled=False):
    width = w_in.shape[0]
    rows = sum(p.shape[0] for p in pieces)
    ins = [w_in, *pieces]
    aliases = {}
    kernel = functools.partial(project_kernel, first, scale, len(pieces), unrolled)
    if table is not None:
        aliases = {len(ins): 0}
        ins.append(table)
    return pl.pallas_call(
        kernel,
        out_shape=jax.ShapeDtypeStruct((total * width // LANES, LANES), jnp.float32),
        in_specs=[VMEM] * len(ins),
        out_specs=VMEM,
        scratch_shapes=[pltpu.VMEM((rows, width), jnp.bfloat16)],
        input_output_aliases=aliases,
        cost_estimate=pl.CostEstimate(
            flops=2 * rows * width * width, bytes_accessed=rows * width * 6, transcendentals=rows * width
        ),
        compiler_params=pltpu.CompilerParams(vmem_limit_bytes=8 << 20),
        name="project",
    )(*ins)


def gate_kernel(count, index_ref, w_ref, *refs):
    pieces, out_ref = refs[:count], refs[-1]
    cand, width = out_ref.shape
    total = jnp.zeros((cand, width), jnp.float32)
    first = 0
    index = jnp.broadcast_to(index_ref[...], (LANES, cand)).T[:, :1]
    for piece in pieces:
        rows = piece.shape[0]
        ids = lax.broadcasted_iota(jnp.int32, (cand, rows), 1) + first
        pick = jnp.where(index == ids, 1.0, 0.0).astype(jnp.bfloat16)
        total = total + jnp.dot(pick, piece[...], preferred_element_type=jnp.float32)
        first += rows
    normed = total.astype(jnp.bfloat16)
    half = 0.5 * jnp.dot(normed, w_ref[:, :width], preferred_element_type=jnp.float32)
    out_ref[...] = half_silu(half).astype(jnp.bfloat16)


def gate_rows(index, pieces, w_in):
    width = w_in.shape[0]
    cand = index.shape[0]
    rows = sum(p.shape[0] for p in pieces)
    return pl.pallas_call(
        functools.partial(gate_kernel, len(pieces)),
        out_shape=jax.ShapeDtypeStruct((cand, width), jnp.bfloat16),
        in_specs=[VMEM] * (2 + len(pieces)),
        out_specs=VMEM,
        cost_estimate=pl.CostEstimate(
            flops=2 * cand * width * (rows + width), bytes_accessed=rows * width * 2, transcendentals=cand * width
        ),
        compiler_params=pltpu.CompilerParams(vmem_limit_bytes=8 << 20),
        name="gate",
    )(index[None, :], w_in, *pieces)


def attend_kernel(sizes, unroll, index_ref, count_ref, block_ref, order_ref, table_ref, k_ref, v_ref, *refs):
    outs, (rows_ref, query_ref, sum_ref, weight_ref) = refs[: len(sizes)], refs[len(sizes) :]
    rows, width = sum_ref.shape
    cuts = width // LANES
    low = lax.broadcasted_iota(jnp.int32, (BLK, LANES), 1) < LANES // 2

    def split(tile):
        zero = jnp.zeros_like(tile)
        return jnp.concatenate([jnp.where(low, tile, zero), jnp.where(low, zero, tile)], axis=0)

    def task(j, carry):
        scorer = order_ref[2 * j]
        start = order_ref[2 * j + 1]
        blocks = count_ref[scorer]
        sum_ref[...] = jnp.zeros_like(sum_ref)

        @pl.when(blocks > 0)
        def _():
            def fetch(i, inner_carry):
                begin = start + i * unroll
                to = i * (unroll * cuts)
                for k in range(unroll):
                    at = pl.multiple_of(index_ref[begin + k], cuts)
                    rows_ref[pl.ds(pl.multiple_of(to + k * cuts, cuts), cuts), :] = table_ref[pl.ds(at, cuts), :]
                return inner_carry

            lax.fori_loop(0, rows // unroll, fetch, 0)
            for c in range(cuts):
                query_ref[:, c * LANES : (c + 1) * LANES] = rows_ref[pl.ds(c, rows, stride=cuts), :].astype(jnp.bfloat16)

            def one_block(slot, inner_carry):
                begin = pl.multiple_of(block_ref[2 * scorer + slot] * BLK, BLK)
                for c in range(cuts):
                    lanes = slice(c * LANES, (c + 1) * LANES)
                    keys = split(k_ref[pl.ds(begin, BLK), lanes])
                    half = lax.dot_general(
                        query_ref[:, lanes], keys, (((1,), (1,)), ((), ())), preferred_element_type=jnp.float32
                    )
                    weight_ref[c] = half_silu(half).astype(jnp.bfloat16)
                for c in range(cuts):
                    lanes = slice(c * LANES, (c + 1) * LANES)
                    values = split(v_ref[pl.ds(begin, BLK), lanes])
                    sum_ref[:, lanes] += jnp.dot(weight_ref[c], values, preferred_element_type=jnp.float32)
                return inner_carry

            lax.fori_loop(0, blocks, one_block, 0)

        at = 0
        for out_ref, number in zip(outs, sizes):
            here = j - at

            @pl.when((here >= 0) & (here < number))
            def _(out_ref=out_ref, here=here):
                out_ref[here] = sum_ref[...].astype(out_ref.dtype)

            at += number
        return carry

    lax.fori_loop(0, sum(sizes), task, 0)


def attend(sizes, rows, index, count, block, order, table, keys, values):
    width = keys.shape[1]
    number = sum(sizes)
    return pl.pallas_call(
        functools.partial(attend_kernel, tuple(sizes), math.gcd(rows, 32)),
        out_shape=[jax.ShapeDtypeStruct((n, rows, width), jnp.bfloat16) for n in sizes],
        in_specs=[SMEM] * 4 + [VMEM] * 3,
        out_specs=[VMEM] * len(sizes),
        scratch_shapes=[
            pltpu.VMEM((rows * width // LANES, LANES), jnp.float32),
            pltpu.VMEM((rows, width), jnp.bfloat16),
            pltpu.VMEM((rows, width), jnp.float32),
            pltpu.VMEM((width // LANES, rows, 2 * BLK), jnp.bfloat16),
        ],
        cost_estimate=pl.CostEstimate(
            flops=number * rows * BLK * width * 8,
            bytes_accessed=number * rows * width * 4,
            transcendentals=number * rows * BLK * H // 2,
        ),
        compiler_params=pltpu.CompilerParams(vmem_limit_bytes=6 << 20),
        name="attend",
    )(index, count, block, order, table, keys, values)


def finish_kernel(halves, *refs):
    gate_ref, w_ref, out_ref = refs[-3], refs[-2], refs[-1]
    at, first = 0, 0
    for number in halves:
        total = refs[at][...].astype(jnp.float32)
        for ref in refs[at + 1 : at + number]:
            total = total + ref[...].astype(jnp.float32)
        rows = total.shape[0]
        gated = (layer_norm(total) * gate_ref[first : first + rows, :].astype(jnp.float32)).astype(jnp.bfloat16)
        out_ref[first : first + rows, :] = jnp.dot(
            gated, w_ref[...], preferred_element_type=jnp.float32
        ).astype(out_ref.dtype)
        at += number
        first += rows


def finish(halves, gate_u, w_out):
    terms = [t for half in halves for t in half]
    return pl.pallas_call(
        functools.partial(finish_kernel, [len(half) for half in halves]),
        out_shape=jax.ShapeDtypeStruct(gate_u.shape, jnp.bfloat16),
        in_specs=[VMEM] * (len(terms) + 2),
        out_specs=VMEM,
        compiler_params=pltpu.CompilerParams(vmem_limit_bytes=8 << 20),
        name="finish",
    )(*terms, gate_u, w_out)


def add(*terms):
    total = terms[0].astype(jnp.float32)
    for term in terms[1:]:
        total = total + term.astype(jnp.float32)
    return total.astype(jnp.bfloat16)


def compute(cand_table, inverse, cache_keys, cache_values, block_dest, w_in, w_out):
    width = w_out.shape[0]
    cand = inverse.shape[0]
    groups, peers = lax.axis_size("grp"), lax.axis_size("shard")
    nx, nz = groups // CORES, peers // NY
    g, s = lax.axis_index("grp"), lax.axis_index("shard")
    part_rows = cand_table.shape[0]
    total_rows = groups * part_rows
    cuts = width // LANES

    def x_shift(value, k):
        return lax.ppermute(
            value, "grp", [(x * CORES + c, (x + k) % nx * CORES + c) for x in range(nx) for c in range(CORES)]
        )

    def swap(value):
        return lax.ppermute(
            value, "grp", [(x * CORES + c, x * CORES + 1 - c) for x in range(nx) for c in range(CORES)]
        )

    def z_shift(value, k):
        return lax.ppermute(
            value, "shard", [(y * nz + z, y * nz + (z + k) % nz) for y in range(NY) for z in range(nz)]
        )

    def y_shift(value, k):
        return lax.ppermute(
            value, "shard", [(y * nz + z, (y + k) % NY * nz + z) for y in range(NY) for z in range(nz)]
        )

    normed = norm(cand_table)
    ahead = x_shift(normed, -1)
    behind = x_shift(normed, 1)
    other = swap(normed)
    wanted = inverse
    step = 1
    while step < nz:
        wanted = jnp.concatenate([wanted, z_shift(wanted, -step)])
        step *= 2
    wanted, ahead, behind = lax.optimization_barrier((wanted, ahead, behind))
    far = x_shift(ahead, -1)
    ahead_rows = [ahead, swap(ahead)]
    behind_rows = [behind, swap(behind)]
    step = 1
    while step < NY:
        wanted = jnp.concatenate([wanted, y_shift(wanted, -step)])
        step *= 2

    def arrival(row):
        owner = row // part_rows
        place = (owner // CORES + nx - g // CORES) & (nx - 1)
        return (place * CORES + ((owner ^ g) & (CORES - 1))) * part_rows + row % part_rows

    index = arrival(wanted) * cuts
    own_relative = arrival(inverse)

    destination = block_dest[:, 0]
    blocks = destination.shape[0]
    block_ids = jnp.arange(blocks, dtype=jnp.int32)
    earlier = (destination[:, None] == destination[None, :]) & (block_ids[None, :] < block_ids[:, None])
    rank = jnp.sum(earlier.astype(jnp.int32), axis=1)
    rel_dest = ((destination // nz + NY - s // nz) & (NY - 1)) * nz + ((destination + nz - s) & (nz - 1))
    slots = jnp.arange(2 * peers, dtype=jnp.int32)
    match = (rel_dest * 2 + rank)[None, :] == slots[:, None]
    block = jnp.sum(jnp.where(match, block_ids[None, :], 0), axis=1)
    count = jnp.sum(
        (rel_dest[None, :] == jnp.arange(peers, dtype=jnp.int32)[:, None]).astype(jnp.int32), axis=1
    )

    scale = 0.5 / math.sqrt(width // H)
    chip = CORES * part_rows
    near_rows = [normed, other]
    table = project(None, 0, total_rows, near_rows, w_in, scale)
    table = project(table, 1 * chip, total_rows, ahead_rows, w_in, scale)
    table = project(table, 3 * chip, total_rows, behind_rows, w_in, scale)
    far_rows = [far, swap(far)]
    table = project(table, 2 * chip, total_rows, far_rows, w_in, scale, unrolled=True)

    half = cand // 2
    half_z = nz // 2
    z_of = lambda dz, dys=range(NY): [(dy, dz, 0) for dy in dys]
    y_of = lambda dy, dzs=range(nz): [(dy, dz, half) for dz in dzs]
    calls = [
        [z_of(4, (0, 1)), z_of(4, (2, 3))],
        [y_of(2, range(half_z)), y_of(2, range(half_z, nz))],
        [z_of(3), z_of(5)],
        [y_of(1), y_of(3)],
        [z_of(2), z_of(6)],
        [z_of(1), z_of(7), z_of(0), y_of(0)],
    ]
    flat = [t for call in calls for piece in call for t in piece]
    order = [v for dy, dz, start in flat for v in (dy * nz + dz, (dy * nz + dz) * cand + start)]
    parts, at = [], 0
    for call in calls:
        sizes = [len(piece) for piece in call]
        mine = jnp.asarray(order[2 * at : 2 * (at + sum(sizes))], jnp.int32)
        parts += attend(sizes, half, index, count, block, mine, table, cache_keys, cache_values)
        at += sum(sizes)
    z4a, z4b, y2a, y2b, z3, z5, y1, y3, z2, z6, z1, z7, z0, y0 = parts

    two = NY // 2
    up = z_shift(z4a, 1)
    down = z_shift(z4b, -1)
    far_y_up = y_shift(y2a, 1)
    far_y_down = y_shift(y2b, -1)
    up = jnp.concatenate([add(up, z3[:two]), z3[two:]], axis=0)
    down = jnp.concatenate([z5[:two], add(down, z5[two:])], axis=0)
    up = z_shift(up, 1)
    down = z_shift(down, -1)
    y_up = jnp.concatenate([add(far_y_up, y1[:half_z]), y1[half_z:]], axis=0)
    y_down = jnp.concatenate([y3[:half_z], add(far_y_down, y3[half_z:])], axis=0)
    y_up = y_shift(y_up, 1)
    y_down = y_shift(y_down, -1)
    up = z_shift(add(up, z2), 1)
    down = z_shift(add(down, z6), -1)
    up = z_shift(add(up, z1), 1)
    down = z_shift(add(down, z7), -1)

    quarter = half // 2

    def y_sum(dz, rows):
        return [y0[dz, rows], y_up[dz, rows], y_down[dz, rows]]

    first, last = slice(0, quarter), slice(quarter, half)
    both = slice(0, half)
    y_first = z_shift(add(*y_sum(4, first)), 1)
    y_last = z_shift(add(*y_sum(4, last)), -1)
    y_first = z_shift(jnp.concatenate([add(y_first, *y_sum(3, first)), add(*y_sum(3, last))], axis=0), 1)
    y_last = z_shift(jnp.concatenate([add(*y_sum(5, first)), add(y_last, *y_sum(5, last))], axis=0), -1)
    for k in (2, 1):
        y_first = z_shift(add(y_first, *y_sum(k, both)), 1)
        y_last = z_shift(add(y_last, *y_sum(nz - k, both)), -1)

    def z_sum(dy, rows):
        return [z0[dy, rows], up[dy, rows], down[dy, rows]]

    z_first = y_shift(add(*z_sum(2, first)), 1)
    z_last = y_shift(add(*z_sum(2, last)), -1)
    z_first = y_shift(jnp.concatenate([add(z_first, *z_sum(1, first)), add(*z_sum(1, last))], axis=0), 1)
    z_last = y_shift(jnp.concatenate([add(*z_sum(3, first)), add(z_last, *z_sum(3, last))], axis=0), -1)

    gate_u = gate_rows(own_relative, near_rows + ahead_rows + far_rows + behind_rows, w_in)
    return finish(
        [[*z_sum(0, both), z_first, z_last], [*y_sum(0, both), y_first, y_last]], gate_u, w_out
    )


def solution(mesh):
    in_specs = (
        P("grp", None),
        P(("grp", "shard")),
        P(("grp", "shard"), None),
        P(("grp", "shard"), None),
        P(("grp", "shard"), None),
        P(),
        P(),
    )
    out_specs = P(("grp", "shard"), None)
    return jax.shard_map(compute, mesh=mesh, in_specs=in_specs, out_specs=out_specs, check_vma=False)
```

```python
import functools
import math

import jax
import jax.numpy as jnp
from jax import lax
from jax.experimental import pallas as pl
from jax.experimental.pallas import tpu as pltpu
from jax.sharding import PartitionSpec as P

H = 8
BLK = 128
LANES = 128
NY = 4
CORES = 2
TILE = 256


VMEM = pl.BlockSpec(memory_space=pltpu.VMEM)
SMEM = pl.BlockSpec(memory_space=pltpu.SMEM)


def layer_norm(inputs):
    center = inputs - jnp.mean(inputs, axis=-1, keepdims=True)
    spread = jnp.mean(center * center, axis=-1, keepdims=True)
    return center * lax.rsqrt(spread + 1e-05)


def half_silu(half):
    return half + half * jnp.tanh(half)


def norm_kernel(in_ref, out_ref):
    tile = math.gcd(in_ref.shape[0], TILE)

    def step(i, carry):
        rows = pl.ds(pl.multiple_of(i * tile, tile), tile)
        out_ref[rows, :] = layer_norm(in_ref[rows, :].astype(jnp.float32)).astype(out_ref.dtype)
        return carry

    lax.fori_loop(0, in_ref.shape[0] // tile, step, 0)


def norm(rows):
    return pl.pallas_call(
        norm_kernel,
        out_shape=jax.ShapeDtypeStruct(rows.shape, jnp.bfloat16),
        in_specs=[VMEM],
        out_specs=VMEM,
        compiler_params=pltpu.CompilerParams(vmem_limit_bytes=8 << 20),
        name="norm",
    )(rows)


def pack_rows(pieces, rows_ref):
    at = 0
    for piece in pieces:
        tile = math.gcd(piece.shape[0], LANES)

        def step(i, carry, piece=piece, at=at, tile=tile):
            begin = pl.multiple_of(i * tile, tile)
            rows_ref[pl.ds(at + begin, tile), :] = piece[pl.ds(begin, tile), :]
            return carry

        lax.fori_loop(0, piece.shape[0] // tile, step, 0)
        at += piece.shape[0]


def halve_kernel(w_ref, out_ref):
    out_ref[...] = w_ref[:, out_ref.shape[1] :]


def query_weights(w_in):
    width = w_in.shape[0]
    return pl.pallas_call(
        halve_kernel,
        out_shape=jax.ShapeDtypeStruct((width, width), w_in.dtype),
        in_specs=[VMEM],
        out_specs=VMEM,
        compiler_params=pltpu.CompilerParams(vmem_limit_bytes=8 << 20),
        name="halve",
    )(w_in)


def project_kernel(first, scale, count, unrolled, *refs):
    w_ref = refs[0]
    out_ref, rows_ref = refs[-2], refs[-1]
    rows, width = rows_ref.shape
    cuts = width // LANES
    tile = math.gcd(refs[1].shape[0], TILE)

    def one_tile(values, to):
        half = 0.5 * jnp.dot(values, w_ref[...], preferred_element_type=jnp.float32)
        query = half_silu(half).astype(jnp.bfloat16).astype(jnp.float32) * scale
        for c in range(cuts):
            out_ref[pl.ds((first + to) * cuts + c, tile, stride=cuts), :] = query[:, c * LANES : (c + 1) * LANES]

    if unrolled:
        at = 0
        for piece in refs[1 : 1 + count]:
            for begin in range(0, piece.shape[0], tile):
                one_tile(piece[begin : begin + tile, :], at + begin)
            at += piece.shape[0]
        return
    pack_rows(refs[1 : 1 + count], rows_ref)

    def step(i, carry):
        begin = pl.multiple_of(i * tile, tile)
        one_tile(rows_ref[pl.ds(begin, tile), :], begin)
        return carry

    lax.fori_loop(0, rows // tile, step, 0)


def project(table, first, total, pieces, w_query, scale, unrolled=False):
    width = w_query.shape[0]
    rows = sum(p.shape[0] for p in pieces)
    ins = [w_query, *pieces]
    aliases = {}
    kernel = functools.partial(project_kernel, first, scale, len(pieces), unrolled)
    if table is not None:
        aliases = {len(ins): 0}
        ins.append(table)
    return pl.pallas_call(
        kernel,
        out_shape=jax.ShapeDtypeStruct((total * width // LANES, LANES), jnp.float32),
        in_specs=[VMEM] * len(ins),
        out_specs=VMEM,
        scratch_shapes=[pltpu.VMEM((rows, width), jnp.bfloat16)],
        input_output_aliases=aliases,
        cost_estimate=pl.CostEstimate(
            flops=2 * rows * width * width, bytes_accessed=rows * width * 6, transcendentals=rows * width
        ),
        compiler_params=pltpu.CompilerParams(vmem_limit_bytes=8 << 20),
        name="project",
    )(*ins)


def gate_kernel(count, index_ref, w_ref, *refs):
    pieces, out_ref = refs[:count], refs[-1]
    cand, width = out_ref.shape
    total = jnp.zeros((cand, width), jnp.float32)
    first = 0
    index = jnp.broadcast_to(index_ref[...], (LANES, cand)).T[:, :1]
    for piece in pieces:
        rows = piece.shape[0]
        ids = lax.broadcasted_iota(jnp.int32, (cand, rows), 1) + first
        pick = jnp.where(index == ids, 1.0, 0.0).astype(jnp.bfloat16)
        total = total + jnp.dot(pick, piece[...], preferred_element_type=jnp.float32)
        first += rows
    normed = total.astype(jnp.bfloat16)
    half = 0.5 * jnp.dot(normed, w_ref[:, :width], preferred_element_type=jnp.float32)
    out_ref[...] = half_silu(half).astype(jnp.bfloat16)


def gate_rows(index, pieces, w_in):
    width = w_in.shape[0]
    cand = index.shape[0]
    rows = sum(p.shape[0] for p in pieces)
    return pl.pallas_call(
        functools.partial(gate_kernel, len(pieces)),
        out_shape=jax.ShapeDtypeStruct((cand, width), jnp.bfloat16),
        in_specs=[VMEM] * (2 + len(pieces)),
        out_specs=VMEM,
        cost_estimate=pl.CostEstimate(
            flops=2 * cand * width * (rows + width), bytes_accessed=rows * width * 2, transcendentals=cand * width
        ),
        compiler_params=pltpu.CompilerParams(vmem_limit_bytes=8 << 20),
        name="gate",
    )(index[None, :], w_in, *pieces)


def attend_kernel(sizes, unroll, index_ref, count_ref, block_ref, order_ref, table_ref, k_ref, v_ref, *refs):
    outs, (rows_ref, query_ref, sum_ref, weight_ref) = refs[: len(sizes)], refs[len(sizes) :]
    rows, width = sum_ref.shape
    cuts = width // LANES
    low = lax.broadcasted_iota(jnp.int32, (BLK, LANES), 1) < LANES // 2

    def split(tile):
        zero = jnp.zeros_like(tile)
        return jnp.concatenate([jnp.where(low, tile, zero), jnp.where(low, zero, tile)], axis=0)

    def task(j, carry):
        scorer = order_ref[2 * j]
        start = order_ref[2 * j + 1]
        blocks = count_ref[scorer]
        sum_ref[...] = jnp.zeros_like(sum_ref)

        @pl.when(blocks > 0)
        def _():
            def fetch(i, inner_carry):
                begin = start + i * unroll
                to = i * (unroll * cuts)
                for k in range(unroll):
                    at = pl.multiple_of(index_ref[begin + k], cuts)
                    rows_ref[pl.ds(pl.multiple_of(to + k * cuts, cuts), cuts), :] = table_ref[pl.ds(at, cuts), :]
                return inner_carry

            lax.fori_loop(0, rows // unroll, fetch, 0)
            for c in range(cuts):
                query_ref[:, c * LANES : (c + 1) * LANES] = rows_ref[pl.ds(c, rows, stride=cuts), :].astype(jnp.bfloat16)

            def one_block(slot, inner_carry):
                begin = pl.multiple_of(block_ref[2 * scorer + slot] * BLK, BLK)
                for c in range(cuts):
                    lanes = slice(c * LANES, (c + 1) * LANES)
                    keys = split(k_ref[pl.ds(begin, BLK), lanes])
                    half = lax.dot_general(
                        query_ref[:, lanes], keys, (((1,), (1,)), ((), ())), preferred_element_type=jnp.float32
                    )
                    weight_ref[c] = half_silu(half).astype(jnp.bfloat16)
                for c in range(cuts):
                    lanes = slice(c * LANES, (c + 1) * LANES)
                    values = split(v_ref[pl.ds(begin, BLK), lanes])
                    sum_ref[:, lanes] += jnp.dot(weight_ref[c], values, preferred_element_type=jnp.float32)
                return inner_carry

            lax.fori_loop(0, blocks, one_block, 0)

        at = 0
        for out_ref, number in zip(outs, sizes):
            here = j - at

            @pl.when((here >= 0) & (here < number))
            def _(out_ref=out_ref, here=here):
                out_ref[here] = sum_ref[...].astype(out_ref.dtype)

            at += number
        return carry

    lax.fori_loop(0, sum(sizes), task, 0)


def attend(sizes, rows, index, count, block, order, table, keys, values):
    width = keys.shape[1]
    number = sum(sizes)
    return pl.pallas_call(
        functools.partial(attend_kernel, tuple(sizes), math.gcd(rows, 32)),
        out_shape=[jax.ShapeDtypeStruct((n, rows, width), jnp.bfloat16) for n in sizes],
        in_specs=[SMEM] * 4 + [VMEM] * 3,
        out_specs=[VMEM] * len(sizes),
        scratch_shapes=[
            pltpu.VMEM((rows * width // LANES, LANES), jnp.float32),
            pltpu.VMEM((rows, width), jnp.bfloat16),
            pltpu.VMEM((rows, width), jnp.float32),
            pltpu.VMEM((width // LANES, rows, 2 * BLK), jnp.bfloat16),
        ],
        cost_estimate=pl.CostEstimate(
            flops=number * rows * BLK * width * 8,
            bytes_accessed=number * rows * width * 4,
            transcendentals=number * rows * BLK * H // 2,
        ),
        compiler_params=pltpu.CompilerParams(vmem_limit_bytes=6 << 20),
        name="attend",
    )(index, count, block, order, table, keys, values)


def finish_kernel(halves, *refs):
    gate_ref, w_ref, out_ref = refs[-3], refs[-2], refs[-1]
    at, first = 0, 0
    for number in halves:
        total = refs[at][...].astype(jnp.float32)
        for ref in refs[at + 1 : at + number]:
            total = total + ref[...].astype(jnp.float32)
        rows = total.shape[0]
        gated = (layer_norm(total) * gate_ref[first : first + rows, :].astype(jnp.float32)).astype(jnp.bfloat16)
        out_ref[first : first + rows, :] = jnp.dot(
            gated, w_ref[...], preferred_element_type=jnp.float32
        ).astype(out_ref.dtype)
        at += number
        first += rows


def finish(halves, gate_u, w_out):
    terms = [t for half in halves for t in half]
    return pl.pallas_call(
        functools.partial(finish_kernel, [len(half) for half in halves]),
        out_shape=jax.ShapeDtypeStruct(gate_u.shape, jnp.bfloat16),
        in_specs=[VMEM] * (len(terms) + 2),
        out_specs=VMEM,
        compiler_params=pltpu.CompilerParams(vmem_limit_bytes=8 << 20),
        name="finish",
    )(*terms, gate_u, w_out)


def add(*terms):
    total = terms[0].astype(jnp.float32)
    for term in terms[1:]:
        total = total + term.astype(jnp.float32)
    return total.astype(jnp.bfloat16)


def compute(cand_table, inverse, cache_keys, cache_values, block_dest, w_in, w_out):
    width = w_out.shape[0]
    cand = inverse.shape[0]
    groups, peers = lax.axis_size("grp"), lax.axis_size("shard")
    nx, nz = groups // CORES, peers // NY
    g, s = lax.axis_index("grp"), lax.axis_index("shard")
    part_rows = cand_table.shape[0]
    total_rows = groups * part_rows
    cuts = width // LANES

    def x_shift(value, k):
        return lax.ppermute(
            value, "grp", [(x * CORES + c, (x + k) % nx * CORES + c) for x in range(nx) for c in range(CORES)]
        )

    def swap(value):
        return lax.ppermute(
            value, "grp", [(x * CORES + c, x * CORES + 1 - c) for x in range(nx) for c in range(CORES)]
        )

    def z_shift(value, k):
        return lax.ppermute(
            value, "shard", [(y * nz + z, y * nz + (z + k) % nz) for y in range(NY) for z in range(nz)]
        )

    def y_shift(value, k):
        return lax.ppermute(
            value, "shard", [(y * nz + z, (y + k) % NY * nz + z) for y in range(NY) for z in range(nz)]
        )

    normed = norm(cand_table)
    w_query = query_weights(w_in)
    ahead = x_shift(normed, -1)
    behind = x_shift(normed, 1)
    other = swap(normed)
    wanted = inverse
    step = 1
    while step < nz:
        wanted = jnp.concatenate([wanted, z_shift(wanted, -step)])
        step *= 2
    far = x_shift(ahead, -1)
    ahead_rows = [ahead, swap(ahead)]
    behind_rows = [behind, swap(behind)]
    step = 1
    while step < NY:
        wanted = jnp.concatenate([wanted, y_shift(wanted, -step)])
        step *= 2

    def arrival(row):
        owner = row // part_rows
        place = (owner // CORES + nx - g // CORES) & (nx - 1)
        return (place * CORES + ((owner ^ g) & (CORES - 1))) * part_rows + row % part_rows

    index = arrival(wanted) * cuts
    own_relative = arrival(inverse)

    destination = block_dest[:, 0]
    blocks = destination.shape[0]
    block_ids = jnp.arange(blocks, dtype=jnp.int32)
    earlier = (destination[:, None] == destination[None, :]) & (block_ids[None, :] < block_ids[:, None])
    rank = jnp.sum(earlier.astype(jnp.int32), axis=1)
    rel_dest = ((destination // nz + NY - s // nz) & (NY - 1)) * nz + ((destination + nz - s) & (nz - 1))
    slots = jnp.arange(2 * peers, dtype=jnp.int32)
    match = (rel_dest * 2 + rank)[None, :] == slots[:, None]
    block = jnp.sum(jnp.where(match, block_ids[None, :], 0), axis=1)
    count = jnp.sum(
        (rel_dest[None, :] == jnp.arange(peers, dtype=jnp.int32)[:, None]).astype(jnp.int32), axis=1
    )

    scale = 0.5 / math.sqrt(width // H)
    chip = CORES * part_rows
    near_rows = [normed, other]
    table = project(None, 0, total_rows, near_rows, w_query, scale)
    table = project(table, 1 * chip, total_rows, ahead_rows, w_query, scale)
    table = project(table, 3 * chip, total_rows, behind_rows, w_query, scale)
    far_rows = [far, swap(far)]
    table = project(table, 2 * chip, total_rows, far_rows, w_query, scale, unrolled=True)

    half = cand // 2
    half_z = nz // 2
    z_of = lambda dz, dys=range(NY): [(dy, dz, 0) for dy in dys]
    y_of = lambda dy, dzs=range(nz): [(dy, dz, half) for dz in dzs]
    calls = [
        [z_of(4, (0, 1)), z_of(4, (2, 3)), y_of(2, range(half_z)), y_of(2, range(half_z, nz))],
        [z_of(3), z_of(5)],
        [y_of(1), y_of(3)],
        [z_of(2), z_of(6)],
        [z_of(1), z_of(7), z_of(0), y_of(0)],
    ]
    flat = [t for call in calls for piece in call for t in piece]
    order = [v for dy, dz, start in flat for v in (dy * nz + dz, (dy * nz + dz) * cand + start)]
    parts, at = [], 0
    for call in calls:
        sizes = [len(piece) for piece in call]
        mine = jnp.asarray(order[2 * at : 2 * (at + sum(sizes))], jnp.int32)
        parts += attend(sizes, half, index, count, block, mine, table, cache_keys, cache_values)
        at += sum(sizes)
    z4a, z4b, y2a, y2b, z3, z5, y1, y3, z2, z6, z1, z7, z0, y0 = parts

    two = NY // 2
    up = z_shift(z4a, 1)
    down = z_shift(z4b, -1)
    far_y_up = y_shift(y2a, 1)
    far_y_down = y_shift(y2b, -1)
    up = jnp.concatenate([add(up, z3[:two]), z3[two:]], axis=0)
    down = jnp.concatenate([z5[:two], add(down, z5[two:])], axis=0)
    up = z_shift(up, 1)
    down = z_shift(down, -1)
    y_up = jnp.concatenate([add(far_y_up, y1[:half_z]), y1[half_z:]], axis=0)
    y_down = jnp.concatenate([y3[:half_z], add(far_y_down, y3[half_z:])], axis=0)
    y_up = y_shift(y_up, 1)
    y_down = y_shift(y_down, -1)
    up = z_shift(add(up, z2), 1)
    down = z_shift(add(down, z6), -1)
    up = z_shift(add(up, z1), 1)
    down = z_shift(add(down, z7), -1)

    quarter = half // 2

    def y_sum(dz, rows):
        return [y0[dz, rows], y_up[dz, rows], y_down[dz, rows]]

    first, last = slice(0, quarter), slice(quarter, half)
    both = slice(0, half)
    y_first = z_shift(add(*y_sum(4, first)), 1)
    y_last = z_shift(add(*y_sum(4, last)), -1)
    y_first = z_shift(jnp.concatenate([add(y_first, *y_sum(3, first)), add(*y_sum(3, last))], axis=0), 1)
    y_last = z_shift(jnp.concatenate([add(*y_sum(5, first)), add(y_last, *y_sum(5, last))], axis=0), -1)
    for k in (2, 1):
        y_first = z_shift(add(y_first, *y_sum(k, both)), 1)
        y_last = z_shift(add(y_last, *y_sum(nz - k, both)), -1)

    def z_sum(dy, rows):
        return [z0[dy, rows], up[dy, rows], down[dy, rows]]

    z_first = y_shift(add(*z_sum(2, first)), 1)
    z_last = y_shift(add(*z_sum(2, last)), -1)
    z_first = y_shift(jnp.concatenate([add(z_first, *z_sum(1, first)), add(*z_sum(1, last))], axis=0), 1)
    z_last = y_shift(jnp.concatenate([add(*z_sum(3, first)), add(z_last, *z_sum(3, last))], axis=0), -1)

    gate_u = gate_rows(own_relative, near_rows + ahead_rows + far_rows + behind_rows, w_in)
    return finish(
        [[*z_sum(0, both), z_first, z_last], [*y_sum(0, both), y_first, y_last]], gate_u, w_out
    )


def solution(mesh):
    in_specs = (
        P("grp", None),
        P(("grp", "shard")),
        P(("grp", "shard"), None),
        P(("grp", "shard"), None),
        P(("grp", "shard"), None),
        P(),
        P(),
    )
    out_specs = P(("grp", "shard"), None)
    return jax.shard_map(compute, mesh=mesh, in_specs=in_specs, out_specs=out_specs, check_vma=False)
```

```python
import functools
import math

import jax
import jax.numpy as jnp
from jax import lax
from jax.experimental import pallas as pl
from jax.experimental.pallas import tpu as pltpu
from jax.sharding import PartitionSpec as P

H = 8
BLK = 128
LANES = 128
NY = 4
CORES = 2
TILE = 256


VMEM = pl.BlockSpec(memory_space=pltpu.VMEM)
SMEM = pl.BlockSpec(memory_space=pltpu.SMEM)


def layer_norm(inputs):
    center = inputs - jnp.mean(inputs, axis=-1, keepdims=True)
    spread = jnp.mean(center * center, axis=-1, keepdims=True)
    return center * lax.rsqrt(spread + 1e-05)


def half_silu(half):
    return half + half * jnp.tanh(half)


def norm_kernel(in_ref, out_ref):
    tile = math.gcd(in_ref.shape[0], TILE)

    def step(i, carry):
        rows = pl.ds(pl.multiple_of(i * tile, tile), tile)
        out_ref[rows, :] = layer_norm(in_ref[rows, :].astype(jnp.float32)).astype(out_ref.dtype)
        return carry

    lax.fori_loop(0, in_ref.shape[0] // tile, step, 0)


def norm(rows):
    return pl.pallas_call(
        norm_kernel,
        out_shape=jax.ShapeDtypeStruct(rows.shape, jnp.bfloat16),
        in_specs=[VMEM],
        out_specs=VMEM,
        compiler_params=pltpu.CompilerParams(vmem_limit_bytes=8 << 20),
        name="norm",
    )(rows)


def pack_rows(pieces, rows_ref):
    at = 0
    for piece in pieces:
        tile = math.gcd(piece.shape[0], LANES)

        def step(i, carry, piece=piece, at=at, tile=tile):
            begin = pl.multiple_of(i * tile, tile)
            rows_ref[pl.ds(at + begin, tile), :] = piece[pl.ds(begin, tile), :]
            return carry

        lax.fori_loop(0, piece.shape[0] // tile, step, 0)
        at += piece.shape[0]


def halve_kernel(w_ref, out_ref):
    out_ref[...] = w_ref[:, out_ref.shape[1] :]


def query_weights(w_in):
    width = w_in.shape[0]
    return pl.pallas_call(
        halve_kernel,
        out_shape=jax.ShapeDtypeStruct((width, width), w_in.dtype),
        in_specs=[VMEM],
        out_specs=VMEM,
        compiler_params=pltpu.CompilerParams(vmem_limit_bytes=8 << 20),
        name="halve",
    )(w_in)


def project_kernel(first, scale, count, unrolled, *refs):
    w_ref = refs[0]
    out_ref, rows_ref = refs[-2], refs[-1]
    rows, width = rows_ref.shape
    cuts = width // LANES
    tile = math.gcd(refs[1].shape[0], TILE)

    def one_tile(values, to):
        half = 0.5 * jnp.dot(values, w_ref[...], preferred_element_type=jnp.float32)
        query = half_silu(half).astype(jnp.bfloat16).astype(jnp.float32) * scale
        for c in range(cuts):
            out_ref[pl.ds((first + to) * cuts + c, tile, stride=cuts), :] = query[:, c * LANES : (c + 1) * LANES]

    if unrolled:
        at = 0
        for piece in refs[1 : 1 + count]:
            for begin in range(0, piece.shape[0], tile):
                one_tile(piece[begin : begin + tile, :], at + begin)
            at += piece.shape[0]
        return
    pack_rows(refs[1 : 1 + count], rows_ref)

    def step(i, carry):
        begin = pl.multiple_of(i * tile, tile)
        one_tile(rows_ref[pl.ds(begin, tile), :], begin)
        return carry

    lax.fori_loop(0, rows // tile, step, 0)


def project(table, first, total, pieces, w_query, scale, unrolled=False):
    width = w_query.shape[0]
    rows = sum(p.shape[0] for p in pieces)
    ins = [w_query, *pieces]
    aliases = {}
    kernel = functools.partial(project_kernel, first, scale, len(pieces), unrolled)
    if table is not None:
        aliases = {len(ins): 0}
        ins.append(table)
    return pl.pallas_call(
        kernel,
        out_shape=jax.ShapeDtypeStruct((total * width // LANES, LANES), jnp.float32),
        in_specs=[VMEM] * len(ins),
        out_specs=VMEM,
        scratch_shapes=[pltpu.VMEM((rows, width), jnp.bfloat16)],
        input_output_aliases=aliases,
        cost_estimate=pl.CostEstimate(
            flops=2 * rows * width * width, bytes_accessed=rows * width * 6, transcendentals=rows * width
        ),
        compiler_params=pltpu.CompilerParams(vmem_limit_bytes=8 << 20),
        name="project",
    )(*ins)


def gate_kernel(count, index_ref, w_ref, *refs):
    pieces, out_ref = refs[:count], refs[-1]
    cand, width = out_ref.shape
    total = jnp.zeros((cand, width), jnp.float32)
    first = 0
    index = jnp.broadcast_to(index_ref[...], (LANES, cand)).T[:, :1]
    for piece in pieces:
        rows = piece.shape[0]
        ids = lax.broadcasted_iota(jnp.int32, (cand, rows), 1) + first
        pick = jnp.where(index == ids, 1.0, 0.0).astype(jnp.bfloat16)
        total = total + jnp.dot(pick, piece[...], preferred_element_type=jnp.float32)
        first += rows
    normed = total.astype(jnp.bfloat16)
    half = 0.5 * jnp.dot(normed, w_ref[:, :width], preferred_element_type=jnp.float32)
    out_ref[...] = half_silu(half).astype(jnp.bfloat16)


def gate_rows(index, pieces, w_in):
    width = w_in.shape[0]
    cand = index.shape[0]
    rows = sum(p.shape[0] for p in pieces)
    return pl.pallas_call(
        functools.partial(gate_kernel, len(pieces)),
        out_shape=jax.ShapeDtypeStruct((cand, width), jnp.bfloat16),
        in_specs=[VMEM] * (2 + len(pieces)),
        out_specs=VMEM,
        cost_estimate=pl.CostEstimate(
            flops=2 * cand * width * (rows + width), bytes_accessed=rows * width * 2, transcendentals=cand * width
        ),
        compiler_params=pltpu.CompilerParams(vmem_limit_bytes=8 << 20),
        name="gate",
    )(index[None, :], w_in, *pieces)


def attend_kernel(sizes, unroll, index_ref, count_ref, block_ref, order_ref, table_ref, k_ref, v_ref, *refs):
    outs, (rows_ref, query_ref, sum_ref, weight_ref) = refs[: len(sizes)], refs[len(sizes) :]
    rows, width = sum_ref.shape
    cuts = width // LANES
    low = lax.broadcasted_iota(jnp.int32, (BLK, LANES), 1) < LANES // 2

    def split(tile):
        zero = jnp.zeros_like(tile)
        return jnp.concatenate([jnp.where(low, tile, zero), jnp.where(low, zero, tile)], axis=0)

    def task(j, carry):
        scorer = order_ref[2 * j]
        start = order_ref[2 * j + 1]
        blocks = count_ref[scorer]
        sum_ref[...] = jnp.zeros_like(sum_ref)

        @pl.when(blocks > 0)
        def _():
            def fetch(i, inner_carry):
                begin = start + i * unroll
                to = i * (unroll * cuts)
                for k in range(unroll):
                    at = pl.multiple_of(index_ref[begin + k], cuts)
                    rows_ref[pl.ds(pl.multiple_of(to + k * cuts, cuts), cuts), :] = table_ref[pl.ds(at, cuts), :]
                return inner_carry

            lax.fori_loop(0, rows // unroll, fetch, 0)
            for c in range(cuts):
                query_ref[:, c * LANES : (c + 1) * LANES] = rows_ref[pl.ds(c, rows, stride=cuts), :].astype(jnp.bfloat16)

            def one_block(slot, inner_carry):
                begin = pl.multiple_of(block_ref[2 * scorer + slot] * BLK, BLK)
                for c in range(cuts):
                    lanes = slice(c * LANES, (c + 1) * LANES)
                    keys = split(k_ref[pl.ds(begin, BLK), lanes])
                    half = lax.dot_general(
                        query_ref[:, lanes], keys, (((1,), (1,)), ((), ())), preferred_element_type=jnp.float32
                    )
                    weight_ref[c] = half_silu(half).astype(jnp.bfloat16)
                for c in range(cuts):
                    lanes = slice(c * LANES, (c + 1) * LANES)
                    values = split(v_ref[pl.ds(begin, BLK), lanes])
                    sum_ref[:, lanes] += jnp.dot(weight_ref[c], values, preferred_element_type=jnp.float32)
                return inner_carry

            lax.fori_loop(0, blocks, one_block, 0)

        at = 0
        for out_ref, number in zip(outs, sizes):
            here = j - at

            @pl.when((here >= 0) & (here < number))
            def _(out_ref=out_ref, here=here):
                out_ref[here] = sum_ref[...].astype(out_ref.dtype)

            at += number
        return carry

    lax.fori_loop(0, sum(sizes), task, 0)


def attend(sizes, rows, index, count, block, order, table, keys, values):
    width = keys.shape[1]
    number = sum(sizes)
    return pl.pallas_call(
        functools.partial(attend_kernel, tuple(sizes), math.gcd(rows, 32)),
        out_shape=[jax.ShapeDtypeStruct((n, rows, width), jnp.bfloat16) for n in sizes],
        in_specs=[SMEM] * 4 + [VMEM] * 3,
        out_specs=[VMEM] * len(sizes),
        scratch_shapes=[
            pltpu.VMEM((rows * width // LANES, LANES), jnp.float32),
            pltpu.VMEM((rows, width), jnp.bfloat16),
            pltpu.VMEM((rows, width), jnp.float32),
            pltpu.VMEM((width // LANES, rows, 2 * BLK), jnp.bfloat16),
        ],
        cost_estimate=pl.CostEstimate(
            flops=number * rows * BLK * width * 8,
            bytes_accessed=number * rows * width * 4,
            transcendentals=number * rows * BLK * H // 2,
        ),
        compiler_params=pltpu.CompilerParams(vmem_limit_bytes=6 << 20),
        name="attend",
    )(index, count, block, order, table, keys, values)


def finish_kernel(halves, *refs):
    gate_ref, w_ref, out_ref = refs[-3], refs[-2], refs[-1]
    at, first = 0, 0
    for number in halves:
        total = refs[at][...].astype(jnp.float32)
        for ref in refs[at + 1 : at + number]:
            total = total + ref[...].astype(jnp.float32)
        rows = total.shape[0]
        gated = (layer_norm(total) * gate_ref[first : first + rows, :].astype(jnp.float32)).astype(jnp.bfloat16)
        out_ref[first : first + rows, :] = jnp.dot(
            gated, w_ref[...], preferred_element_type=jnp.float32
        ).astype(out_ref.dtype)
        at += number
        first += rows


def finish(halves, gate_u, w_out):
    terms = [t for half in halves for t in half]
    return pl.pallas_call(
        functools.partial(finish_kernel, [len(half) for half in halves]),
        out_shape=jax.ShapeDtypeStruct(gate_u.shape, jnp.bfloat16),
        in_specs=[VMEM] * (len(terms) + 2),
        out_specs=VMEM,
        compiler_params=pltpu.CompilerParams(vmem_limit_bytes=8 << 20),
        name="finish",
    )(*terms, gate_u, w_out)


def add(*terms):
    total = terms[0].astype(jnp.float32)
    for term in terms[1:]:
        total = total + term.astype(jnp.float32)
    return total.astype(jnp.bfloat16)


def compute(cand_table, inverse, cache_keys, cache_values, block_dest, w_in, w_out):
    width = w_out.shape[0]
    cand = inverse.shape[0]
    groups, peers = lax.axis_size("grp"), lax.axis_size("shard")
    nx, nz = groups // CORES, peers // NY
    g, s = lax.axis_index("grp"), lax.axis_index("shard")
    part_rows = cand_table.shape[0]
    total_rows = groups * part_rows
    cuts = width // LANES

    def x_shift(value, k):
        return lax.ppermute(
            value, "grp", [(x * CORES + c, (x + k) % nx * CORES + c) for x in range(nx) for c in range(CORES)]
        )

    def swap(value):
        return lax.ppermute(
            value, "grp", [(x * CORES + c, x * CORES + 1 - c) for x in range(nx) for c in range(CORES)]
        )

    def z_shift(value, k):
        return lax.ppermute(
            value, "shard", [(y * nz + z, y * nz + (z + k) % nz) for y in range(NY) for z in range(nz)]
        )

    def y_shift(value, k):
        return lax.ppermute(
            value, "shard", [(y * nz + z, (y + k) % NY * nz + z) for y in range(NY) for z in range(nz)]
        )

    normed = norm(cand_table)
    w_query = query_weights(w_in)
    ahead = x_shift(normed, -1)
    behind = x_shift(normed, 1)
    other = swap(normed)
    wanted = inverse
    step = 1
    while step < nz:
        wanted = jnp.concatenate([wanted, z_shift(wanted, -step)])
        step *= 2
    far = x_shift(ahead, -1)
    ahead_rows = [ahead, swap(ahead)]
    behind_rows = [behind, swap(behind)]
    step = 1
    while step < NY:
        wanted = jnp.concatenate([wanted, y_shift(wanted, -step)])
        step *= 2

    def arrival(row):
        owner = row // part_rows
        place = (owner // CORES + nx - g // CORES) & (nx - 1)
        return (place * CORES + ((owner ^ g) & (CORES - 1))) * part_rows + row % part_rows

    index = arrival(wanted) * cuts
    own_relative = arrival(inverse)

    destination = block_dest[:, 0]
    blocks = destination.shape[0]
    block_ids = jnp.arange(blocks, dtype=jnp.int32)
    earlier = (destination[:, None] == destination[None, :]) & (block_ids[None, :] < block_ids[:, None])
    rank = jnp.sum(earlier.astype(jnp.int32), axis=1)
    rel_dest = ((destination // nz + NY - s // nz) & (NY - 1)) * nz + ((destination + nz - s) & (nz - 1))
    slots = jnp.arange(2 * peers, dtype=jnp.int32)
    match = (rel_dest * 2 + rank)[None, :] == slots[:, None]
    block = jnp.sum(jnp.where(match, block_ids[None, :], 0), axis=1)
    count = jnp.sum(
        (rel_dest[None, :] == jnp.arange(peers, dtype=jnp.int32)[:, None]).astype(jnp.int32), axis=1
    )

    scale = 0.5 / math.sqrt(width // H)
    chip = CORES * part_rows
    near_rows = [normed, other]
    table = project(None, 0, total_rows, near_rows, w_query, scale, unrolled=True)
    table = project(table, 1 * chip, total_rows, ahead_rows, w_query, scale, unrolled=True)
    table = project(table, 3 * chip, total_rows, behind_rows, w_query, scale, unrolled=True)
    far_rows = [far, swap(far)]
    table = project(table, 2 * chip, total_rows, far_rows, w_query, scale, unrolled=True)

    half = cand // 2
    half_z = nz // 2
    z_of = lambda dz, dys=range(NY): [(dy, dz, 0) for dy in dys]
    y_of = lambda dy, dzs=range(nz): [(dy, dz, half) for dz in dzs]
    calls = [
        [z_of(4, (0, 1)), z_of(4, (2, 3)), y_of(2, range(half_z)), y_of(2, range(half_z, nz))],
        [z_of(3), z_of(5)],
        [y_of(1), y_of(3)],
        [z_of(2), z_of(6)],
        [z_of(1), z_of(7), z_of(0), y_of(0)],
    ]
    flat = [t for call in calls for piece in call for t in piece]
    order = [v for dy, dz, start in flat for v in (dy * nz + dz, (dy * nz + dz) * cand + start)]
    parts, at = [], 0
    for call in calls:
        sizes = [len(piece) for piece in call]
        mine = jnp.asarray(order[2 * at : 2 * (at + sum(sizes))], jnp.int32)
        parts += attend(sizes, half, index, count, block, mine, table, cache_keys, cache_values)
        at += sum(sizes)
    z4a, z4b, y2a, y2b, z3, z5, y1, y3, z2, z6, z1, z7, z0, y0 = parts

    two = NY // 2
    up = z_shift(z4a, 1)
    down = z_shift(z4b, -1)
    far_y_up = y_shift(y2a, 1)
    far_y_down = y_shift(y2b, -1)
    up = jnp.concatenate([add(up, z3[:two]), z3[two:]], axis=0)
    down = jnp.concatenate([z5[:two], add(down, z5[two:])], axis=0)
    up = z_shift(up, 1)
    down = z_shift(down, -1)
    y_up = jnp.concatenate([add(far_y_up, y1[:half_z]), y1[half_z:]], axis=0)
    y_down = jnp.concatenate([y3[:half_z], add(far_y_down, y3[half_z:])], axis=0)
    y_up = y_shift(y_up, 1)
    y_down = y_shift(y_down, -1)
    up = z_shift(add(up, z2), 1)
    down = z_shift(add(down, z6), -1)
    up = z_shift(add(up, z1), 1)
    down = z_shift(add(down, z7), -1)

    quarter = half // 2

    def y_sum(dz, rows):
        return [y0[dz, rows], y_up[dz, rows], y_down[dz, rows]]

    first, last = slice(0, quarter), slice(quarter, half)
    both = slice(0, half)
    y_first = z_shift(add(*y_sum(4, first)), 1)
    y_last = z_shift(add(*y_sum(4, last)), -1)
    y_first = z_shift(jnp.concatenate([add(y_first, *y_sum(3, first)), add(*y_sum(3, last))], axis=0), 1)
    y_last = z_shift(jnp.concatenate([add(*y_sum(5, first)), add(y_last, *y_sum(5, last))], axis=0), -1)
    for k in (2, 1):
        y_first = z_shift(add(y_first, *y_sum(k, both)), 1)
        y_last = z_shift(add(y_last, *y_sum(nz - k, both)), -1)

    def z_sum(dy, rows):
        return [z0[dy, rows], up[dy, rows], down[dy, rows]]

    z_first = y_shift(add(*z_sum(2, first)), 1)
    z_last = y_shift(add(*z_sum(2, last)), -1)
    z_first = y_shift(jnp.concatenate([add(z_first, *z_sum(1, first)), add(*z_sum(1, last))], axis=0), 1)
    z_last = y_shift(jnp.concatenate([add(*z_sum(3, first)), add(z_last, *z_sum(3, last))], axis=0), -1)

    gate_u = gate_rows(own_relative, near_rows + ahead_rows + far_rows + behind_rows, w_in)
    return finish(
        [[*z_sum(0, both), z_first, z_last], [*y_sum(0, both), y_first, y_last]], gate_u, w_out
    )


def solution(mesh):
    in_specs = (
        P("grp", None),
        P(("grp", "shard")),
        P(("grp", "shard"), None),
        P(("grp", "shard"), None),
        P(("grp", "shard"), None),
        P(),
        P(),
    )
    out_specs = P(("grp", "shard"), None)
    return jax.shard_map(compute, mesh=mesh, in_specs=in_specs, out_specs=out_specs, check_vma=False)
```
